32 devices in a mesh: groups: 2 (over y), tile: 16 (over z, x, core).
Axes of the slice: x: 2, y: 2, z: 4, core: 2. Of those that a mesh axis runs over, the one named last changes fastest.
Arguments:
- sar_faces: bfloat16 [512, 8, 128], P(('groups', 'tile')), parts along dimension 0, may hold values from -6 to 6
- dest_owner: int32 [512, 1], P(('groups', 'tile')), parts along dimension 0, may hold values from 0 to 15; in each aligned block of 16 rows (0 to 15, 16 to 31, ...) at most 2 rows name the same one
- face_slot: int32 [512], P(('groups', 'tile')), parts along dimension 0, may hold values from 0 to 31
- valid_pixels: int32 [512], P(('groups', 'tile')), parts along dimension 0, may hold values from 1 to 8
- cloud_mask: int32 [32, 256], P(('groups', 'tile')), parts along dimension 0, may hold values 0 or 1
- time_index: int32 [32], P(('groups', 'tile')), parts along dimension 0, may hold values from 0 to 999
- clean_latent: bfloat16 [32, 256, 384], P(('groups', 'tile')), parts along dimension 0, may hold values from -6 to 6
- noise_latent: bfloat16 [32, 256, 384], P(('groups', 'tile')), parts along dimension 0, may hold values from -6 to 6
- encoder_first: bfloat16 [3, 8, 16, 48], replicated, may hold values from -0.875 to 0.875
- encoder_second: bfloat16 [3, 8, 48, 48], replicated, may hold values from -0.5 to 0.5
- conv_kernel: bfloat16 [9, 384, 384], replicated, may hold values from -0.109375 to 0.109375
- norm_gain: float32 [384], replicated, may hold values from 0.5 to 2
Outputs:
- grad_kernel: float32 [18, 384, 384], P('groups'), parts along dimension 0
- grad_gain: float32 [768], P('groups'), parts along dimension 0
- grad_first: float32 [6, 8, 16, 48], P('groups'), parts along dimension 0
- grad_second: float32 [6, 8, 48, 48], P('groups'), parts along dimension 0
The draws below stay inside these ranges and needn't reach their ends.
There are 2 independent parts, one for each index of `groups`. The reference program is written for one: setup_inputs(seed, part) draws one part's arguments, and reference() takes and returns one part's arrays. A program takes and returns all parts, laid end to end along the dimension named above; an argument that names none is the same for every part. Nothing has to cross between parts.
Inputs may be any that keep to these rules, and one draw needn't show every extreme that they name: `dest_owner`: among each device's 16 faces, at most 2 name one tile owner.
All inputs are finite; a program needn't handle non-finite values. No bound on the sum of `cloud_mask` on one device may be relied on, other than what follows from the above.
Results may differ from the reference program's by a relative error of at most 0.0038.
Values may be sent and summed in bfloat16 or wider, within the bound.
A program may use at most 64 MiB of HBM per device.

```python
import math
import jax
import jax.numpy as jnp
import numpy as np
from jax import lax

C = 384
CIN = 128
G = 8
LINE = 8
MOST = 2
COLS = 256
NSTEPS = 1000
FACES_DEV = 16
TILES = 16
SCENE_ROWS = 16
FACES = 256
TILE_FACES = 32
N_TILE = 16


def plant(drawn, key, low, largest):
    shape = drawn.shape
    spot = [jax.random.randint(jax.random.fold_in(key, axis), (), 0, shape[axis]) for axis in range(len(shape))]
    drawn = drawn.at[tuple(spot)].set(low)
    longest = shape.index(max(shape))
    spot[longest] = (spot[longest] + 1) % shape[longest]
    return drawn.at[tuple(spot)].set(largest)


def block_scale(key, extent, split, low, largest):
    def one(dim, blocks):
        steps = jax.random.uniform(jax.random.fold_in(jax.random.fold_in(key, 6), dim), (blocks,), jnp.float32, low / len(split), largest / len(split))
        return jnp.repeat(jnp.exp(steps), extent[dim] // blocks).reshape((-1,) + (1,) * (len(extent) - dim - 1))

    factor_of = one(*split[0])
    for cut in split[1:]:
        factor_of = factor_of * one(*cut)
    return factor_of


def routed_block(stream_key, own, number, rows, number_of, top, most, lean):
    sequence = jax.random.permutation(stream_key, number_of)
    packed, usual = load_shares(number_of, rows * top, most, lean, True), load_shares(number_of, rows * top, most, lean, False)
    places = jnp.arange(number_of)

    def named(tallies, rotation):
        used = int((tallies > 0).sum())
        fixed = max(1, used // 4)
        moved = fixed + (places - fixed + rotation * (used - fixed)) % max(1, number_of - fixed)
        return jnp.zeros((number_of,), jnp.int32).at[sequence[jnp.where(places < fixed, places, moved)]].set(jnp.asarray(tallies, jnp.int32))

    tallies = jnp.where(number % 4 == 0, named(packed, number // 4), named(usual, number - number // 4 - 1))
    mixed = jax.random.permutation(jax.random.fold_in(own, 3), number_of)
    giver, receiver = mixed[0:number_of // 2 * 2:2], mixed[1:number_of // 2 * 2:2]
    room = jnp.minimum(tallies[giver] - 1, most - tallies[receiver]) // 2
    room = jnp.where((giver == sequence[0]) | (receiver == sequence[0]) | (tallies[receiver] == 0), 0, jnp.maximum(room, 0))
    moved = jax.random.randint(jax.random.fold_in(own, 4), (number_of // 2,), 0, 1 << 20) % (room + 1)
    tallies = tallies.at[giver].add(-moved).at[receiver].add(moved)
    items = jnp.searchsorted(jnp.cumsum(tallies), jnp.arange(rows * top), side="right").astype(jnp.int32)
    table = items.reshape(top, rows).T
    table = table[jax.random.permutation(jax.random.fold_in(own, 1), rows)]
    rotation = jax.random.randint(jax.random.fold_in(own, 2), (rows, 1), 0, top)
    return jnp.take_along_axis(table, (jnp.arange(top)[None, :] + rotation) % top, axis=1)


def load_shares(amount, total, bound, lean, full):
    weights = [(1 << 20) // math.isqrt(standing ** lean) + 1 for standing in range(1, amount + 1)]
    largest = bound if full else min(bound, max(-(-total // amount), total * weights[0] // sum(weights)))
    least = 1 if total - largest >= amount - 1 else 0
    counts, surplus = [largest] + [least] * (amount - 1), total - largest - least * (amount - 1)
    while surplus > 0:
        free = [i for i in range(1, amount) if counts[i] < largest] or [i for i in range(1, amount) if counts[i] < bound]
        pool, left = sum([weights[i] for i in free]), surplus
        for i in free:
            extra = min(bound - counts[i], max(1, left * weights[i] // pool), surplus)
            counts[i] = counts[i] + extra
            surplus = surplus - extra
    return np.array(counts)


def noise(stream_key, shape, scale, limit, cuts=(), kind=jnp.bfloat16):
    result = scale * jax.random.normal(stream_key, shape, jnp.float32)
    if cuts:
        result = result * block_scale(stream_key, shape, cuts, -0.22, 0.18)
    return jnp.clip(result, -limit, limit).astype(kind)


def setup_inputs(seed: int = 0, part: int = 0) -> dict:
    seeds = jax.random.split(jax.random.key(seed), 13)
    own_keys = jax.random.split(jax.random.fold_in(seeds[12], part), 13)
    sar_faces = noise(own_keys[0], (FACES, LINE, CIN), 1.0, 6.0, ((0, 16),))
    dest_owner_keys = jax.random.split(jax.random.fold_in(own_keys[1], 1), FACES // FACES_DEV)
    dest_owner_turns = jax.random.permutation(jax.random.fold_in(own_keys[1], 3), FACES // FACES_DEV)
    dest_owner = jax.vmap(lambda own, number: routed_block(jax.random.fold_in(own_keys[1], 2), own, number, FACES_DEV, N_TILE, 1, MOST, 2))(dest_owner_keys, dest_owner_turns).reshape((FACES, 1))
    face_slot = plant(jax.random.randint(own_keys[2], (FACES,), 0, TILE_FACES), jax.random.fold_in(own_keys[2], 1), 0, TILE_FACES - 1).astype(jnp.int32)
    valid_pixels = plant(jax.random.randint(own_keys[3], (FACES,), 1, LINE + 1), jax.random.fold_in(own_keys[3], 1), 1, LINE).astype(jnp.int32)
    cloud_mask = plant((jax.random.randint(own_keys[4], (SCENE_ROWS, COLS), 0, 3) < 1).astype(jnp.int32), jax.random.fold_in(own_keys[4], 1), 0, 1)
    time_index = plant(jax.random.randint(own_keys[5], (TILES,), 0, NSTEPS), jax.random.fold_in(own_keys[5], 1), 0, NSTEPS - 1).astype(jnp.int32)
    clean_latent = noise(own_keys[6], (SCENE_ROWS, COLS, C), 1.0, 6.0, ((0, 16),))
    noise_latent = noise(own_keys[7], (SCENE_ROWS, COLS, C), 1.0, 6.0, ((0, 16),))
    encoder_first = noise(seeds[8], (3, G, CIN // G, C // G), (3 * CIN // G) ** -0.5, 0.875)
    encoder_second = noise(seeds[9], (3, G, C // G, C // G), (3 * C // G) ** -0.5, 0.5)
    conv_kernel = noise(seeds[10], (9, C, C), (9 * C) ** -0.5, 0.109375)
    norm_gain = jnp.clip(jnp.exp(jax.random.uniform(seeds[11], (C,), jnp.float32, math.log(0.5), math.log(2.0))), 0.5, 2.0)
    return {"sar_faces": sar_faces, "dest_owner": dest_owner, "face_slot": face_slot, "valid_pixels": valid_pixels, "cloud_mask": cloud_mask, "time_index": time_index, "clean_latent": clean_latent, "noise_latent": noise_latent, "encoder_first": encoder_first, "encoder_second": encoder_second, "conv_kernel": conv_kernel, "norm_gain": norm_gain}


highest = lax.Precision.HIGHEST
epsilon = 1e-06

def shift_line(values, offset):
    if offset == 0:
        return values
    zeros = jnp.zeros_like(values[:, :abs(offset)])
    if offset > 0:
        return jnp.concatenate([values[:, offset:], zeros], axis=1)
    return jnp.concatenate([zeros, values[:, :offset]], axis=1)

def grouped_taps(inputs, weight, spread):
    summed = jnp.zeros(inputs.shape[:3] + (weight.shape[-1],), jnp.float32)
    for shift_tap in range(3):
        shifted = shift_line(inputs, (shift_tap - 1) * spread)
        summed = summed + jnp.einsum('flgi,gio->flgo', shifted, weight[shift_tap], precision=highest)
    return summed

def encoder(sar_faces, first_w, second_w):
    face_count, length, channels_in = sar_faces.shape
    groups = first_w.shape[1]
    inputs = sar_faces.astype(jnp.float32).reshape(face_count, length, groups, -1)
    hidden = jax.nn.silu(grouped_taps(inputs, first_w, 1)).reshape(face_count, length, -1)
    hidden = lax.optimization_barrier(hidden.astype(jnp.bfloat16)).astype(jnp.float32)
    second = grouped_taps(hidden.reshape(face_count, length, groups, -1), second_w, 2)
    return (hidden + second.reshape(face_count, length, -1)).astype(jnp.bfloat16)

def convolve_forward(padded, kernel, rows, columns):
    channels = kernel.shape[-1]
    summed = jnp.zeros((rows * columns, channels), jnp.float32)
    for row_tap in range(3):
        for col_tap in range(3):
            window = padded[row_tap:row_tap + rows, col_tap:col_tap + columns].reshape(-1, channels)
            summed = summed + jnp.dot(window, kernel[3 * row_tap + col_tap], preferred_element_type=jnp.float32)
    return summed

def convolve_backward(padded_act, padded_grad, kernel, rows, columns):
    channels = kernel.shape[-1]
    incoming = padded_grad[1:rows + 1, 1:columns + 1].reshape(-1, channels)
    flows = jnp.zeros((rows * columns, channels), jnp.float32)
    kernels = []
    for row_tap in range(3):
        for col_tap in range(3):
            window = padded_act[row_tap:row_tap + rows, col_tap:col_tap + columns].reshape(-1, channels)
            kernels.append(lax.dot_general(window, incoming, (((0,), (0,)), ((), ())), preferred_element_type=jnp.float32))
            moved = padded_grad[2 - row_tap:2 - row_tap + rows, 2 - col_tap:2 - col_tap + columns].reshape(-1, channels)
            flows = flows + lax.dot_general(moved, kernel[3 * row_tap + col_tap], (((1,), (1,)), ((), ())), preferred_element_type=jnp.float32)
    return (flows, jnp.stack(kernels))

def norm_backward(flows, lifted, normed, inverse, gain):
    logistic = jax.nn.sigmoid(lifted)
    grad_lift = flows * logistic * (1.0 + lifted * (1.0 - logistic))
    gain_part = lax.optimization_barrier(jnp.sum(grad_lift * normed, axis=0))
    grad_norm = grad_lift * gain
    grad_hsum = inverse * (grad_norm - normed * lax.optimization_barrier(jnp.mean(grad_norm * normed, axis=-1, keepdims=True)))
    return (gain_part, grad_hsum)

def reference(sar_faces, dest_owner, face_slot, valid_pixels, cloud_mask, time_index, clean_latent, noise_latent, encoder_first, encoder_second, conv_kernel, norm_gain):
    first_w = encoder_first.astype(jnp.float32)
    second_w = encoder_second.astype(jnp.float32)
    encoded, pullback = jax.vjp(lambda one_w, two_w: encoder(sar_faces, one_w, two_w), first_w, second_w)
    length = sar_faces.shape[1]
    tile_count = time_index.shape[0]
    scene_rows, columns, channels = clean_latent.shape
    rows = scene_rows // tile_count
    tile_faces = rows * columns // length
    validity = (jnp.arange(length, dtype=jnp.int32)[None, :] < valid_pixels[:, None]).astype(jnp.float32)
    position = (dest_owner[:, 0] * tile_faces + face_slot).astype(jnp.int32)
    summed = jax.ops.segment_sum(encoded.astype(jnp.float32) * validity[..., None], position, num_segments=tile_count * tile_faces)
    covered = jax.ops.segment_sum(validity, position, num_segments=tile_count * tile_faces)
    covered = covered.reshape(-1, 1)
    condition = summed.reshape(-1, channels) / (1.0 + covered)
    time_value = (time_index.astype(jnp.float32) + 0.5) / NSTEPS
    time_rows = jnp.repeat(time_value, rows * columns)[:, None]
    noise_flat = noise_latent.astype(jnp.float32).reshape(-1, channels)
    clean_flat = clean_latent.astype(jnp.float32).reshape(-1, channels)
    hsum = (1.0 - time_rows) * noise_flat + time_rows * clean_flat + condition
    inverse = lax.rsqrt(lax.optimization_barrier(jnp.mean(hsum * hsum, axis=-1, keepdims=True)) + epsilon)
    normed = hsum * inverse
    lifted = normed * norm_gain
    activated = jax.nn.silu(lifted).astype(jnp.bfloat16).reshape(scene_rows, columns, channels)
    padded = jnp.pad(activated, ((1, 1), (1, 1), (0, 0)))
    predicted = convolve_forward(padded, conv_kernel, scene_rows, columns)
    pixel_weight = (1 + cloud_mask).astype(jnp.float32).reshape(-1, 1)
    grad_pred = (pixel_weight * (predicted - clean_flat + noise_flat) / (rows * columns)).astype(jnp.bfloat16)
    padded_grad = jnp.pad(grad_pred.reshape(scene_rows, columns, channels), ((1, 1), (1, 1), (0, 0)))
    flows, grad_kernel = convolve_backward(padded, padded_grad, conv_kernel, scene_rows, columns)
    grad_gain, grad_hsum = norm_backward(flows, lifted, normed, inverse, norm_gain)
    scaled = (grad_hsum / (1.0 + covered)).reshape(tile_count * tile_faces, length, channels)
    grad_face = (jnp.take(scaled, position, axis=0) * validity[..., None]).astype(jnp.bfloat16)
    grad_first, grad_second = pullback(grad_face)
    return (grad_kernel, grad_gain, grad_first, grad_second)
```

```python
import jax
import jax.numpy as jnp
from jax import lax
from jax.experimental import pallas as pl
from jax.experimental.pallas import tpu as pltpu
from jax.sharding import PartitionSpec as P

MOST = 2
NSTEPS = 1000


highest = lax.Precision.HIGHEST
epsilon = 1e-06


def with_halo(block, sides, width):
    for axis, dim in sides:
        count = lax.axis_size(axis)
        forward = [(i, i + 1) for i in range(count - 1)]
        backward = [(target, source) for source, target in forward]
        low = lax.ppermute(
            lax.slice_in_dim(block, block.shape[dim] - width, None, axis=dim), axis, forward
        )
        high = lax.ppermute(lax.slice_in_dim(block, 0, width, axis=dim), axis, backward)
        block = jnp.concatenate([low, block, high], axis=dim)
    return block


def shift_line(values, offset):
    if offset == 0:
        return values
    zeros = jnp.zeros_like(values[:, : abs(offset)])
    if offset > 0:
        return jnp.concatenate([values[:, offset:], zeros], axis=1)
    return jnp.concatenate([zeros, values[:, :offset]], axis=1)


def taps_forward(inputs, weight, spread):
    summed = jnp.zeros(inputs.shape[:3] + (weight.shape[-1],), jnp.float32)
    for shift_tap in range(3):
        shifted = shift_line(inputs, (shift_tap - 1) * spread)
        summed = summed + jnp.einsum(
            "flgi,gio->flgo", shifted, weight[shift_tap], preferred_element_type=jnp.float32
        )
    return summed


def taps_weight_grad(inputs, cotangent, spread, exact):
    pieces = []
    for shift_tap in range(3):
        shifted = shift_line(inputs, (shift_tap - 1) * spread)
        if exact:
            pieces.append(
                jnp.einsum(
                    "flgi,flgo->gio", shifted.astype(jnp.float32), cotangent, precision=highest
                )
            )
        else:
            pieces.append(
                jnp.einsum("flgi,flgo->gio", shifted, cotangent, preferred_element_type=jnp.float32)
            )
    return jnp.stack(pieces)


def taps_input_grad(cotangent, weight, spread):
    summed = jnp.zeros(cotangent.shape[:3] + (weight.shape[2],), jnp.float32)
    for shift_tap in range(3):
        moved = jnp.einsum(
            "flgo,gio->flgi", cotangent, weight[shift_tap], preferred_element_type=jnp.float32
        )
        summed = summed + shift_line(moved, -(shift_tap - 1) * spread)
    return summed


def encoder_forward(sar_faces, first_w, second_w):
    face_count, length, channels_in = sar_faces.shape
    groups = first_w.shape[1]
    inputs = sar_faces.reshape(face_count, length, groups, -1)
    first_out = taps_forward(inputs, first_w, 1)
    hidden = jax.nn.silu(first_out).astype(jnp.bfloat16)
    second = taps_forward(hidden, second_w, 2)
    encoded = (
        (hidden.astype(jnp.float32) + second).reshape(face_count, length, -1).astype(jnp.bfloat16)
    )
    return (encoded, (inputs, first_out, hidden))


def encoder_backward(saved, grad_face, first_w, second_w):
    inputs, first_out, hidden = saved
    groups = first_w.shape[1]
    face_count, length, channels = grad_face.shape
    cotangent = grad_face.reshape(face_count, length, groups, -1)
    second_part = taps_weight_grad(hidden, cotangent, 2, False)
    grad_hidden = cotangent.astype(jnp.float32) + taps_input_grad(cotangent, second_w, 2)
    logistic = jax.nn.sigmoid(first_out)
    grad_first_out = grad_hidden * logistic * (1.0 + first_out * (1.0 - logistic))
    first_part = taps_weight_grad(inputs, grad_first_out, 1, True)
    return (first_part, second_part)


def convolve_forward(padded, kernel, rows, columns):
    channels = kernel.shape[-1]
    summed = jnp.zeros((rows * columns, channels), jnp.float32)
    for row_tap in range(3):
        for col_tap in range(3):
            window = padded[row_tap : row_tap + rows, col_tap : col_tap + columns].reshape(
                -1, channels
            )
            summed = summed + jnp.dot(
                window, kernel[3 * row_tap + col_tap], preferred_element_type=jnp.float32
            )
    return summed


def convolve_backward(padded_act, padded_grad, kernel, rows, columns):
    channels = kernel.shape[-1]
    incoming = padded_grad[1 : rows + 1, 1 : columns + 1].reshape(-1, channels)
    flows = jnp.zeros((rows * columns, channels), jnp.float32)
    kernels = []
    for row_tap in range(3):
        for col_tap in range(3):
            window = padded_act[row_tap : row_tap + rows, col_tap : col_tap + columns].reshape(
                -1, channels
            )
            kernels.append(
                lax.dot_general(
                    window, incoming, (((0,), (0,)), ((), ())), preferred_element_type=jnp.float32
                )
            )
            moved = padded_grad[
                2 - row_tap : 2 - row_tap + rows, 2 - col_tap : 2 - col_tap + columns
            ].reshape(-1, channels)
            flows = flows + lax.dot_general(
                moved,
                kernel[3 * row_tap + col_tap],
                (((1,), (1,)), ((), ())),
                preferred_element_type=jnp.float32,
            )
    return (flows, jnp.stack(kernels))


def norm_backward(flows, lifted, normed, inverse, gain):
    logistic = jax.nn.sigmoid(lifted)
    grad_lift = flows * logistic * (1.0 + lifted * (1.0 - logistic))
    gain_part = jnp.sum(grad_lift * normed, axis=0)
    grad_norm = grad_lift * gain
    grad_hsum = inverse * (
        grad_norm - normed * jnp.mean(grad_norm * normed, axis=-1, keepdims=True)
    )
    return (gain_part, grad_hsum)


MESH = pl.DeviceIdType.MESH
VM = pltpu.VMEM
ANY = pl.ANY
F32 = jnp.float32
BF16 = jnp.bfloat16
ZERO, CROSS = 17, 16


class Gather:
    def __init__(self, buf, send, recv):
        self.buf, self.send_sem, self.recv_sem = buf, send, recv
        self.me = lax.axis_index("tile")
        self.core = lax.rem(self.me, 2)
        self.x = lax.rem(self.me // 2, 2)
        self.z = z = self.me // 4
        self.x_peer = z * 4 + (1 - self.x) * 2 + self.core
        self.sibling = z * 4 + self.x * 2 + (1 - self.core)
        self.planes = [
            z,
            jnp.where(z == 0, 1, z - 1),
            jnp.where(z == 0, 2, jnp.where(z == 3, 1, z + 1)),
            jnp.where(z < 2, 3, 0),
        ]

    def copy(self, chunk, to, index):
        return pltpu.make_async_remote_copy(
            src_ref=self.buf.at[chunk],
            dst_ref=self.buf.at[chunk],
            send_sem=self.send_sem.at[index],
            recv_sem=self.recv_sem.at[chunk],
            device_id={"tile": to},
            device_id_type=MESH,
        )

    def at(self, step, x, core):
        return self.planes[step] * 4 + x * 2 + core

    def along(self, step):
        place = lax.rem(self.me, 4)
        onward = jnp.where(self.planes[step] < self.z, self.z + 1, self.z - 1)
        valid = (onward >= 0) & (onward <= 3)
        return jnp.clip(onward, 0, 3) * 4 + place, valid

    def start(self):
        place = lax.rem(self.me, 4)

        @pl.when(self.z < 3)
        def _():
            self.copy(self.me, jnp.minimum(self.z + 1, 3) * 4 + place, 0).start()

        @pl.when(self.z > 0)
        def _():
            self.copy(self.me, jnp.maximum(self.z - 1, 0) * 4 + place, 1).start()

        self.copy(self.me, self.x_peer, 2).start()
        self.copy(self.me, self.sibling, 3).start()

    def pass_z(self, step):
        chunk = self.at(step, self.x, self.core)
        self.copy(chunk, self.x_peer, 0).wait_recv()
        to, valid = self.along(step)

        @pl.when(valid)
        def _():
            self.copy(chunk, to, 3 + step).start()

        self.copy(chunk, self.x_peer, 6 + step).start()
        self.copy(chunk, self.sibling, 9 + step).start()

    def pass_x(self, step):
        chunk = self.at(step, 1 - self.x, self.core)
        self.copy(chunk, self.sibling, 0).wait_recv()
        self.copy(chunk, self.sibling, 13 + step).start()

    def take(self, step):
        for x in (self.x, 1 - self.x):
            chunk = self.at(step, x, 1 - self.core)
            self.copy(chunk, self.sibling, 0).wait_recv()

    def drain(self):
        @pl.when(self.z < 3)
        def _():
            self.copy(self.me, self.sibling, 0).wait_send()

        @pl.when(self.z > 0)
        def _():
            self.copy(self.me, self.sibling, 1).wait_send()

        for step in range(1, 4):
            _, valid = self.along(step)

            @pl.when(valid)
            def _():
                self.copy(self.me, self.sibling, 3 + step).wait_send()

        for index in (2, 3, 7, 8, 9, 10, 11, 12, 13, 14, 15, 16):
            self.copy(self.me, self.sibling, index).wait_send()


def moved(values, offset, axis):
    extent = values.shape[axis]
    rolled = pltpu.roll(values, (-offset) % extent, axis)
    place = lax.broadcasted_iota(jnp.int32, values.shape, axis)
    return jnp.where(place == (extent - 1 if offset > 0 else 0), 0.0, rolled)


def iota(shape, axis):
    return lax.broadcasted_iota(jnp.int32, shape, axis)


def over_48(index):
    return ((index >> 4) * 171) >> 9


def along_face(values, offset):
    if offset == 0:
        return values
    rolled = pltpu.roll(values, (-offset) % values.shape[0], 0)
    place = (iota(values.shape, 0) & 7) + offset
    return jnp.where((place >= 0) & (place < 8), rolled, 0.0)


def dot(left, right):
    return jnp.dot(left, right, preferred_element_type=F32)


def dot_back(left, right):
    return lax.dot_general(left, right, (((1,), (1,)), ((), ())), preferred_element_type=F32)


def wide(values):
    return jnp.concatenate([values, values, values], axis=1)


class Crossing:
    def __init__(self, buf, sems):
        me = lax.axis_index("tile")
        place = lax.rem(me, 4)
        self.goes = ((place == 0) & (me > 0)) | ((place == 3) & (me < 15))
        to = jnp.where(place == 0, jnp.maximum(me - 1, 0), jnp.minimum(me + 1, 15))
        self.copy = pltpu.make_async_remote_copy(
            src_ref=buf.at[me],
            dst_ref=buf.at[CROSS],
            send_sem=sems.at[0],
            recv_sem=sems.at[1],
            device_id={"tile": to},
            device_id_type=MESH,
        )
        self.above = jnp.where(place > 0, me - 1, jnp.where(me > 0, CROSS, ZERO))
        self.below = jnp.where(place < 3, me + 1, jnp.where(me < 15, CROSS, ZERO))

    def start(self):
        @pl.when(self.goes)
        def _():
            self.copy.start()

    def wait_recv(self):
        @pl.when(self.goes)
        def _():
            self.copy.wait_recv()

    def wait_send(self):
        @pl.when(self.goes)
        def _():
            self.copy.wait_send()


def step_kernel(
    time_ref,
    owner_hbm,
    slot_hbm,
    count_hbm,
    faces_hbm,
    mask_hbm,
    gain_hbm,
    w1_hbm,
    w2_hbm,
    clean_hbm,
    noise_hbm,
    kernel_hbm,
    acc_ref,
    shifted,
    gbuf,
    small_ref,
    owner_ref,
    slot_ref,
    count_ref,
    faces_ref,
    mask_ref,
    gain_ref,
    w1_ref,
    w2_ref,
    clean_ref,
    noise_ref,
    kernel_ref,
    load_sems,
    sbuf,
    rbuf,
    x_send,
    x_recv,
    w1_dense,
    w2_dense,
    mixed,
    first_out,
    inputs,
    hiddens,
    chosen,
    inv_cov,
    inverse_ref,
    normed_ref,
    act_ref,
    abuf,
    a_send,
    a_recv,
    a_cross,
    g_send,
    g_recv,
    g_cross,
    small_out,
    small_in,
    s_send,
    s_recv,
    t_send,
    t_recv,
    half_send,
    half_recv,
):
    me = lax.axis_index("tile")
    barrier = pltpu.get_barrier_semaphore()
    for k in range(1, 16):
        pl.semaphore_signal(
            barrier, inc=1, device_id={"tile": lax.rem(me + k, 16)}, device_id_type=MESH
        )
    pairs = (
        (owner_hbm, owner_ref),
        (slot_hbm, slot_ref),
        (count_hbm, count_ref),
        (faces_hbm, faces_ref),
        (mask_hbm, mask_ref),
        (gain_hbm, gain_ref),
        (w1_hbm, w1_ref),
        (w2_hbm, w2_ref),
        (clean_hbm, clean_ref),
        (noise_hbm, noise_ref),
        (kernel_hbm, kernel_ref),
    )
    loads = [
        pltpu.make_async_copy(far, near, load_sems.at[i]) for i, (far, near) in enumerate(pairs)
    ]
    for load in loads:
        load.start()
    core = lax.rem(me, 2)
    pixels, channels = act_ref.shape
    faces = owner_ref.shape[1]

    with jax.named_scope("pack"):
        for load in loads[:4]:
            load.wait()
        square = (faces, faces)
        diagonal = iota(square, 0) == iota(square, 1)
        owner_row = owner_ref[...].astype(F32)
        owner_col = jnp.sum(jnp.where(diagonal, owner_row, 0.0), axis=1, keepdims=True)
        earlier = (owner_col == owner_row) & (iota(square, 1) < iota(square, 0))
        within = jnp.sum(jnp.where(earlier, 1.0, 0.0), axis=1, keepdims=True)
        goes_to = owner_col * 16.0 + within * 8.0
        lines = 8 * faces
        of_face = iota((faces, lines), 0) == (iota((faces, lines), 1) >> 3)
        row_of = jnp.sum(jnp.where(of_face, goes_to, 0.0), axis=0, keepdims=True)
        row_of = row_of + (iota((1, lines), 1) & 7).astype(F32)
        packer = jnp.where(iota((256, lines), 0).astype(F32) == row_of, 1.0, 0.0).astype(BF16)
        mine = (iota((lines, faces), 0) >> 3) == iota((lines, faces), 1)
        slot_of = jnp.sum(
            jnp.where(mine, slot_ref[...].astype(F32), 0.0), axis=1, keepdims=True
        )
        count_of = jnp.sum(
            jnp.where(mine, count_ref[...].astype(F32), 0.0), axis=1, keepdims=True
        )
        pixel = (iota((lines, 1), 0) & 7).astype(F32)
        label = jnp.where(pixel < count_of, slot_of * 8.0 + pixel + 1.0, 0.0)
        sbuf[:, 0:16, :] = dot(packer, faces_ref[...]).astype(BF16).reshape(16, 16, 128)
        sbuf[:, 16:32, :] = (
            dot(packer, jnp.broadcast_to(label, (lines, 128)).astype(BF16))
            .astype(BF16)
            .reshape(16, 16, 128)
        )
    with jax.named_scope("barrier"):
        pl.semaphore_wait(barrier, 15)
        sends = []
        for k in range(1, 16):
            to = lax.rem(me + k, 16)
            send = pltpu.make_async_remote_copy(
                src_ref=sbuf.at[to],
                dst_ref=rbuf.at[me],
                send_sem=x_send.at[k - 1],
                recv_sem=x_recv.at[k - 1],
                device_id={"tile": to},
                device_id_type=MESH,
            )
            send.start()
            sends.append(send)
        rbuf[me] = sbuf[me]
    with jax.named_scope("dense"):
        for load in loads[4:]:
            load.wait()
        spread = (
            iota((48, channels), 1) - 48 * over_48(iota((48, channels), 1)) == iota((48, channels), 0)
        )
        spread = jnp.where(spread, 1.0, 0.0).astype(BF16)
        group_of = over_48(iota((1, channels), 1))
        keep1 = (iota((128, 1), 0) >> 4) == group_of
        keep2 = over_48(iota((channels, 1), 0)) == group_of
        for k in range(3):
            dense = dot(w1_ref[k * 128 : (k + 1) * 128], spread)
            w1_dense[k] = jnp.where(keep1, dense, 0.0).astype(BF16)
            dense = dot(w2_ref[k * channels : (k + 1) * channels], spread)
            w2_dense[k] = jnp.where(keep2, dense, 0.0).astype(BF16)
        time_value = (jnp.full((1, channels), time_ref[0], jnp.int32).astype(F32) + 0.5) / NSTEPS
        mixed[...] = (1.0 - time_value) * noise_ref[...].astype(F32) + time_value * clean_ref[
            ...
        ].astype(F32)
        on_diagonal = iota((pixels, pixels), 0) == iota((pixels, pixels), 1)
        cloudy = jnp.where(on_diagonal, mask_ref[...].astype(F32), 0.0).astype(BF16)
        pixel_weight = (1.0 + dot(cloudy, jnp.ones((pixels, 128), BF16))) / pixels
        zero_pixels = jnp.zeros((3 * channels, pixels), BF16)
        shifted[:, 0:pixels] = zero_pixels
        shifted[:, 17 * pixels : 18 * pixels] = zero_pixels
        abuf[ZERO] = jnp.zeros((channels, pixels), BF16)
        gbuf[ZERO] = jnp.zeros((pixels, channels), BF16)
    with jax.named_scope("faces_wait"):
        for send in sends:
            send.wait()
    with jax.named_scope("encoder"):
        plain = rbuf[:, 0:16, :].reshape(256, 128).astype(F32)
        total = jnp.zeros((256, channels), F32)
        for k in range(3):
            inputs[k] = along_face(plain, k - 1).astype(BF16)
            total = total + dot(inputs[k], w1_dense[k])
        first_out[...] = total
        hidden = (total * jax.nn.sigmoid(total)).astype(BF16)
        hidden_wide = hidden.astype(F32)
        total = hidden_wide
        for k in range(3):
            hiddens[k] = along_face(hidden_wide, 2 * (k - 1)).astype(BF16)
            total = total + dot(hiddens[k], w2_dense[k])
        encoded = total.astype(BF16)
        labels = rbuf[:, 16:32, :].reshape(256, 128).astype(F32)
        hits = jnp.concatenate([labels, labels], axis=1) == (iota((256, pixels), 1) + 1).astype(F32)
        chosen[...] = jnp.where(hits, 1.0, 0.0).astype(BF16)
        placer = chosen[...].T
        inv_cov[...] = 1.0 / (1.0 + dot(placer, jnp.ones((256, 128), BF16)))
        hsum = mixed[...] + dot(placer, encoded) * wide(inv_cov[...])
        inverse = lax.rsqrt(jnp.mean(hsum * hsum, axis=1, keepdims=True) + epsilon)
        inverse_ref[...] = jnp.broadcast_to(inverse, (pixels, 128))
        normed_ref[...] = hsum * inverse
        lifted = normed_ref[...] * gain_ref[...]
        act_ref[...] = (lifted * jax.nn.sigmoid(lifted)).astype(BF16)
    with jax.named_scope("act_send"):
        abuf[me] = act_ref[...].T
        acts = Gather(abuf, a_send, a_recv)
        a_row = Crossing(abuf, a_cross)
        a_row.start()
        acts.start()
        own = act_ref[...]
        sums = [dot(own, kernel_ref[3 + d]) for d in range(3)]
    with jax.named_scope("a0"):
        acts.pass_x(0)
        acts.pass_z(1)
        acts.take(0)
    with jax.named_scope("a_row"):
        a_row.wait_recv()
    with jax.named_scope("conv_halo"):
        above = abuf[a_row.above].T
        below = abuf[a_row.below].T
        sums = [
            sums[d] + dot(above, kernel_ref[d]) + dot(below, kernel_ref[6 + d]) for d in range(3)
        ]
        predicted = sums[1] + moved(sums[0], -1, 0) + moved(sums[2], 1, 0)
        grad = (
            wide(pixel_weight)
            * (predicted - clean_ref[...].astype(F32) + noise_ref[...].astype(F32))
        ).astype(BF16)
    with jax.named_scope("g_send"):
        gbuf[me] = grad
        grads = Gather(gbuf, g_send, g_recv)
        g_row = Crossing(gbuf, g_cross)
        g_row.start()
        grads.start()

        def shift_one(chunk):
            plain = abuf[chunk]
            values = plain.astype(F32)
            here = pl.ds(pl.multiple_of((chunk + 1) * pixels, pixels), pixels)
            shifted[0:channels, here] = moved(values, -1, 1).astype(BF16)
            shifted[channels : 2 * channels, here] = plain
            shifted[2 * channels : 3 * channels, here] = moved(values, 1, 1).astype(BF16)

        def shift_plane(order):
            base = acts.planes[order] * 4

            def step(i, carry):
                shift_one(base + i)
                return carry

            lax.fori_loop(0, 4, step, 0)

        part = channels // 2
        half = pl.ds(pl.multiple_of(core * part, part), part)

        def half_copy(row):
            return pltpu.make_async_remote_copy(
                src_ref=acc_ref.at[pl.ds(3 * row, 3), half],
                dst_ref=acc_ref.at[pl.ds(3 * row, 3), half],
                send_sem=half_send.at[row],
                recv_sem=half_recv.at[row],
                device_id={"tile": acts.sibling},
                device_id_type=MESH,
            )

        def multiply(order):
            base = acts.planes[order] * 4
            right = gbuf[pl.ds(base, 4)].reshape(4 * pixels, channels)

            def step(row, carry):
                start = pl.multiple_of((base + row) * pixels, pixels)
                for d in range(3):
                    rows = pl.ds(pl.multiple_of(d * channels + core * part, part), part)
                    piece = dot(shifted[rows, pl.ds(start, 4 * pixels)], right)
                    if order == 0:
                        acc_ref[3 * row + d, half, :] = piece
                    else:
                        acc_ref[3 * row + d, half, :] = acc_ref[3 * row + d, half, :] + piece
                if order == 2:
                    half_copy(row).start()
                return carry

            lax.fori_loop(0, 3, step, 0)
    with jax.named_scope("back_own"):
        own = gbuf[me]
        sums = [dot_back(own, kernel_ref[3 + d]) for d in range(3)]
    with jax.named_scope("relay1"):
        acts.pass_z(2)
        acts.pass_x(1)
        shift_plane(0)
        grads.pass_x(0)
        grads.pass_z(1)
    with jax.named_scope("relay2"):
        acts.pass_z(3)
        grads.take(0)
    with jax.named_scope("g_row"):
        g_row.wait_recv()
    with jax.named_scope("back_halo"):
        above = gbuf[g_row.above]
        below = gbuf[g_row.below]
        sums = [
            sums[d] + dot_back(below, kernel_ref[d]) + dot_back(above, kernel_ref[6 + d])
            for d in range(3)
        ]
        flows = sums[1] + moved(sums[0], 1, 0) + moved(sums[2], -1, 0)
    with jax.named_scope("relay3"):
        acts.pass_x(2)
    with jax.named_scope("norm_back"):
        gain = gain_ref[...]
        normed = normed_ref[...]
        lifted = normed * gain
        logistic = jax.nn.sigmoid(lifted)
        grad_lift = flows * logistic * (1.0 + lifted * (1.0 - logistic))
        gain_part = jnp.sum(grad_lift * normed, axis=0, keepdims=True)
        grad_norm = grad_lift * gain
        grad_hsum = wide(inverse_ref[...]) * (
            grad_norm - normed * jnp.mean(grad_norm * normed, axis=1, keepdims=True)
        )
        scaled = (grad_hsum * wide(inv_cov[...])).astype(BF16)
    with jax.named_scope("relay4"):
        acts.pass_x(3)
    with jax.named_scope("encoder_back"):
        cotangent_wide = dot(chosen[...], scaled)
        cotangent = cotangent_wide.astype(BF16)
        grad_hidden = cotangent_wide
        small_rows = []
        for k in range(3):
            grad_hidden = grad_hidden + dot_back(
                along_face(cotangent_wide, -2 * (k - 1)).astype(BF16), w2_dense[k]
            )
            product = jnp.where(keep2, dot(hiddens[k].T, cotangent), 0.0)
            small_rows.append(sum(product[48 * g : 48 * (g + 1)] for g in range(8)))
        logistic = jax.nn.sigmoid(first_out[...])
        grad_first = grad_hidden * logistic * (1.0 + first_out[...] * (1.0 - logistic))
        grad_high = grad_first.astype(BF16)
        grad_low = (grad_first - grad_high.astype(F32)).astype(BF16)
        for k in range(3):
            turned = inputs[k].T
            product = jnp.where(keep1, dot(turned, grad_high) + dot(turned, grad_low), 0.0)
            small_rows.append(sum(product[16 * g : 16 * (g + 1)] for g in range(8)))
        small_rows.append(
            jnp.where(iota((16, channels), 0) == 0, jnp.broadcast_to(gain_part, (16, channels)), 0.0)
        )
        small_out[...] = jnp.concatenate(small_rows, axis=0).astype(BF16)
    with jax.named_scope("small_send"):
        def small_send(k):
            to = lax.rem(me + k, 16)
            rows = pl.ds(pl.multiple_of(jnp.minimum(to, 12) * 16, 16), 16)
            return to < 13, pltpu.make_async_remote_copy(
                src_ref=small_out.at[rows],
                dst_ref=small_in.at[me],
                send_sem=s_send.at[k - 1],
                recv_sem=s_recv.at[k - 1],
                device_id={"tile": to},
                device_id_type=MESH,
            )

        my_rows = pl.ds(pl.multiple_of(jnp.minimum(me, 12) * 16, 16), 16)

        def small_spread(k):
            return pltpu.make_async_remote_copy(
                src_ref=small_ref.at[my_rows],
                dst_ref=small_ref.at[my_rows],
                send_sem=t_send.at[k - 1],
                recv_sem=t_recv.at[k - 1],
                device_id={"tile": lax.rem(me + k, 16)},
                device_id_type=MESH,
            )

        for k in range(1, 16):
            valid, send = small_send(k)

            @pl.when(valid)
            def _():
                send.start()
    with jax.named_scope("takes"):
        acts.take(1)
        acts.take(2)
        acts.take(3)
        shift_plane(1)
    with jax.named_scope("relay5"):
        grads.pass_z(2)
        grads.pass_x(1)
    with jax.named_scope("mult0"):
        shift_plane(2)
        multiply(0)
    with jax.named_scope("relay6"):
        grads.pass_z(3)
        grads.pass_x(2)
        shift_plane(3)
        grads.take(1)
    with jax.named_scope("small_sum"):
        @pl.when(me < 13)
        def _():
            for k in range(1, 16):
                small_send(k)[1].wait_recv()
            small_in[me] = small_out[my_rows, :]
            added = small_in[0].astype(F32)
            for k in range(1, 16):
                added = added + small_in[k].astype(F32)
            small_ref[my_rows, :] = added.astype(BF16)
            for k in range(1, 16):
                small_spread(k).start()
    with jax.named_scope("mult1"):
        multiply(1)
        grads.pass_x(3)
    with jax.named_scope("take2"):
        grads.take(2)
        multiply(2)
    with jax.named_scope("small_wait"):
        for k in range(1, 16):

            @pl.when(lax.rem(me + 16 - k, 16) < 13)
            def _():
                small_spread(k).wait_recv()
    with jax.named_scope("take3"):
        grads.take(3)
    with jax.named_scope("half_wait"):
        for row in range(3):
            half_copy(row).wait()
    with jax.named_scope("drain"):
        @pl.when(me < 13)
        def _():
            for k in range(1, 16):
                small_spread(k).wait_send()

        for k in range(1, 16):
            valid, send = small_send(k)

            @pl.when(valid)
            def _():
                send.wait_send()

        acts.drain()
        grads.drain()
        a_row.wait_send()
        g_row.wait_send()


def step_call(
    time_index, owner, slot, count, faces, mask, gain, first_w, second_w, clean, noise, kernel
):
    pixels, channels = clean.shape
    dma = pltpu.SemaphoreType.DMA
    whole = pl.BlockSpec(memory_space=VM)
    staged = (owner, slot, count, faces, mask, gain, first_w, second_w, clean, noise, kernel)
    staged = tuple(pltpu.with_memory_space_constraint(array, pltpu.HBM) for array in staged)
    return pl.pallas_call(
        step_kernel,
        out_shape=(
            jax.ShapeDtypeStruct((9, channels, channels), F32),
            jax.ShapeDtypeStruct((3 * channels, 18 * pixels), BF16),
            jax.ShapeDtypeStruct((18, pixels, channels), BF16),
            jax.ShapeDtypeStruct((208, channels), BF16),
        ),
        in_specs=[pl.BlockSpec(memory_space=pltpu.SMEM)]
        + [pl.BlockSpec(memory_space=ANY)] * len(staged),
        out_specs=(whole,) * 4,
        scratch_shapes=[VM(array.shape, array.dtype) for array in staged]
        + [
            dma((len(staged),)),
            VM((16, 32, 128), BF16),
            VM((16, 32, 128), BF16),
            dma((15,)),
            dma((15,)),
            VM((3, 128, channels), BF16),
            VM((3, channels, channels), BF16),
            VM((pixels, channels), F32),
            VM((256, channels), F32),
            VM((3, 256, 128), BF16),
            VM((3, 256, channels), BF16),
            VM((256, pixels), BF16),
            VM((pixels, 128), F32),
            VM((pixels, 128), F32),
            VM((pixels, channels), F32),
            VM((pixels, channels), BF16),
            VM((18, channels, pixels), BF16),
            dma((17,)),
            dma((16,)),
            dma((2,)),
            dma((17,)),
            dma((16,)),
            dma((2,)),
            VM((208, channels), BF16),
            VM((16, 16, channels), BF16),
            dma((15,)),
            dma((15,)),
            dma((15,)),
            dma((15,)),
            dma((3,)),
            dma((3,)),
        ],
        compiler_params=pltpu.CompilerParams(
            collective_id=0, has_side_effects=True, vmem_limit_bytes=28 * 2**20
        ),
        name="step",
    )(time_index, *staged)


def finish_kernel(
    acc_ref, shifted, gbuf, small_ref, kernel_out, gain_out, first_out, second_out, held, sems
):
    me = lax.axis_index("tile")
    channels = acc_ref.shape[1]
    pixels = gbuf.shape[1]
    z = me // 4
    base = 4 * jnp.where(z < 2, 3, 0)
    right = gbuf[pl.ds(base, 4)].reshape(4 * pixels, channels)

    def step(row, carry):
        start = pl.multiple_of((base + row) * pixels, pixels)
        for d in range(3):
            tap = 3 * row + d
            left = shifted[d * channels : (d + 1) * channels, pl.ds(start, 4 * pixels)]
            held[tap] = acc_ref[tap] + dot(left, right)
            pltpu.make_async_copy(held.at[tap], kernel_out.at[tap], sems.at[tap]).start()
        return carry

    lax.fori_loop(0, 3, step, 0)
    summed = small_ref[...].astype(F32)
    for k in range(3):
        second = summed[48 * k : 48 * (k + 1)]
        first = summed[144 + 16 * k : 144 + 16 * (k + 1)]
        for g in range(8):
            turn = (channels - 48 * g) % channels
            turned = pltpu.roll(second, turn, 1)[:, :48] if turn else second[:, :48]
            second_out[(8 * k + g) * 48 : (8 * k + g + 1) * 48, :] = turned
            turned = pltpu.roll(first, turn, 1)[:, :48] if turn else first[:, :48]
            first_out[(8 * k + g) * 16 : (8 * k + g + 1) * 16, :] = turned
    gain_out[...] = summed[192:193]
    for tap in range(9):
        pltpu.make_async_copy(held.at[tap], kernel_out.at[tap], sems.at[tap]).wait()


def finish_call(acc, shifted, grads, small):
    channels = acc.shape[1]
    whole = pl.BlockSpec(memory_space=VM)
    return pl.pallas_call(
        finish_kernel,
        out_shape=(
            jax.ShapeDtypeStruct(acc.shape, F32),
            jax.ShapeDtypeStruct((1, channels), F32),
            jax.ShapeDtypeStruct((384, 48), F32),
            jax.ShapeDtypeStruct((1152, 48), F32),
        ),
        in_specs=[whole] * 4,
        out_specs=(pl.BlockSpec(memory_space=ANY), whole, whole, whole),
        scratch_shapes=[VM(acc.shape, F32), pltpu.SemaphoreType.DMA((9,))],
        compiler_params=pltpu.CompilerParams(vmem_limit_bytes=12 * 2**20),
        name="finish",
    )(acc, shifted, grads, small)


def body16(
    sar_faces,
    dest_owner,
    face_slot,
    valid_pixels,
    cloud_mask,
    time_index,
    clean_latent,
    noise_latent,
    encoder_first,
    encoder_second,
    conv_kernel,
    norm_gain,
):
    channels_in = sar_faces.shape[-1]
    channels = clean_latent.shape[-1]
    acc, shifted, grads, small = step_call(
        time_index,
        dest_owner.reshape(1, -1),
        face_slot.reshape(1, -1),
        valid_pixels.reshape(1, -1),
        sar_faces.reshape(-1, channels_in),
        cloud_mask,
        norm_gain.reshape(1, -1),
        encoder_first.reshape(-1, encoder_first.shape[-1]),
        encoder_second.reshape(-1, encoder_second.shape[-1]),
        clean_latent.reshape(-1, channels),
        noise_latent.reshape(-1, channels),
        conv_kernel,
    )
    grad_kernel, grad_gain, grad_first, grad_second = finish_call(acc, shifted, grads, small)
    return (
        grad_kernel,
        grad_gain.reshape(-1),
        grad_first.reshape(encoder_first.shape),
        grad_second.reshape(encoder_second.shape),
    )


def body(
    sar_faces,
    dest_owner,
    face_slot,
    valid_pixels,
    cloud_mask,
    time_index,
    clean_latent,
    noise_latent,
    encoder_first,
    encoder_second,
    conv_kernel,
    norm_gain,
):
    owners = lax.axis_size("tile")
    slot_total = owners * MOST
    face_count, length, channels_in = sar_faces.shape
    rows, columns, channels = clean_latent.shape
    tile_faces = rows * columns // length
    owner_list = dest_owner[:, 0]
    order = jnp.arange(face_count, dtype=jnp.int32)
    within = jnp.sum(
        (
            (owner_list[:, None] == owner_list[None, :]) & (order[None, :] < order[:, None])
        ).astype(jnp.int32),
        axis=1,
    )
    buffer_at = owner_list * MOST + within
    placed = (jnp.arange(slot_total, dtype=jnp.int32)[:, None] == buffer_at[None, :]).astype(
        jnp.int32
    )
    placer = placed.astype(jnp.bfloat16)
    labels = jnp.stack(
        [
            jnp.sum(placed * face_slot[None, :], axis=1),
            jnp.sum(placed * valid_pixels[None, :], axis=1),
        ],
        axis=-1,
    )
    labels = labels.reshape(owners, MOST, 2)
    packed = jnp.einsum(
        "sf,fjc->sjc", placer, sar_faces, preferred_element_type=jnp.float32
    ).astype(jnp.bfloat16)
    arrived, recv_labels = (
        lax.all_to_all(
            packed.reshape(owners, MOST, length, channels_in),
            "tile",
            split_axis=0,
            concat_axis=0,
            tiled=True,
        ),
        lax.all_to_all(labels, "tile", split_axis=0, concat_axis=0, tiled=True),
    )
    raw_slots = arrived.reshape(slot_total, length, channels_in)
    received, saved = encoder_forward(raw_slots, encoder_first, encoder_second)
    recv_labels = recv_labels.reshape(slot_total, 2)
    recv_slot = recv_labels[:, 0]
    recv_count = recv_labels[:, 1]
    validity = (jnp.arange(length, dtype=jnp.int32)[None, :] < recv_count[:, None]).astype(
        jnp.float32
    )
    selector = recv_slot[:, None] == jnp.arange(tile_faces, dtype=jnp.int32)[None, :]
    masked = received * validity[..., None].astype(jnp.bfloat16)
    summed = jnp.einsum(
        "sp,sjc->pjc", selector.astype(jnp.bfloat16), masked, preferred_element_type=jnp.float32
    )
    covered = jnp.einsum(
        "sp,sj->pj", selector.astype(jnp.float32), validity, precision=highest
    ).reshape(-1, 1)
    condition = summed.reshape(-1, channels) / (1.0 + covered)
    time_value = (time_index[0].astype(jnp.float32) + 0.5) / NSTEPS
    noise_flat = noise_latent.astype(jnp.float32).reshape(-1, channels)
    clean_flat = clean_latent.astype(jnp.float32).reshape(-1, channels)
    hsum = (1.0 - time_value) * noise_flat + time_value * clean_flat + condition
    inverse = lax.rsqrt(jnp.mean(hsum * hsum, axis=-1, keepdims=True) + epsilon)
    normed = hsum * inverse
    lifted = normed * norm_gain
    activated = jax.nn.silu(lifted).astype(jnp.bfloat16).reshape(rows, columns, channels)
    extended = with_halo(activated, (("tile", 0),), 1)
    padded = jnp.pad(extended, ((0, 0), (1, 1), (0, 0)))
    predicted = convolve_forward(padded, conv_kernel, rows, columns)
    pixel_weight = (1 + cloud_mask).astype(jnp.float32).reshape(-1, 1)
    grad_pred = (pixel_weight * (predicted - clean_flat + noise_flat) / (rows * columns)).astype(
        jnp.bfloat16
    )
    grad_rows = with_halo(grad_pred.reshape(rows, columns, channels), (("tile", 0),), 1)
    padded_grad = jnp.pad(grad_rows, ((0, 0), (1, 1), (0, 0)))
    flows, kernel_part = convolve_backward(padded, padded_grad, conv_kernel, rows, columns)
    gain_part, grad_hsum = norm_backward(flows, lifted, normed, inverse, norm_gain)
    scaled = (grad_hsum / (1.0 + covered)).astype(jnp.bfloat16)
    target = recv_slot[:, None] * length + jnp.arange(length, dtype=jnp.int32)[None, :]
    target = jnp.where(validity > 0, target, -1).reshape(-1)
    picker = target[:, None] == jnp.arange(rows * columns, dtype=jnp.int32)[None, :]
    slot_grads = jnp.dot(
        picker.astype(jnp.bfloat16), scaled, preferred_element_type=jnp.float32
    ).astype(jnp.bfloat16)
    slot_grads = slot_grads.reshape(slot_total, length, channels)
    first_part, second_part = encoder_backward(saved, slot_grads, encoder_first, encoder_second)
    reduced = lax.psum((kernel_part, gain_part, first_part, second_part), "tile")
    return (reduced[0], reduced[1], reduced[2], reduced[3])


def solution(mesh):
    placed = (
        P(("groups", "tile"), None, None),
        P(("groups", "tile"), None),
        P(("groups", "tile")),
        P(("groups", "tile")),
        P(("groups", "tile"), None),
        P(("groups", "tile")),
        P(("groups", "tile"), None, None),
        P(("groups", "tile"), None, None),
        P(),
        P(),
        P(),
        P(),
    )
    return jax.shard_map(
        body16 if mesh.shape["tile"] == 16 else body,
        mesh=mesh,
        in_specs=placed,
        out_specs=(
            P("groups", None, None),
            P("groups"),
            P("groups", None, None, None),
            P("groups", None, None, None),
        ),
        check_vma=False,
    )
```

```python
import jax
import jax.numpy as jnp
from jax import lax
from jax.experimental import pallas as pl
from jax.experimental.pallas import tpu as pltpu
from jax.sharding import PartitionSpec as P

MOST = 2
NSTEPS = 1000


highest = lax.Precision.HIGHEST
epsilon = 1e-06


def with_halo(block, sides, width):
    for axis, dim in sides:
        count = lax.axis_size(axis)
        forward = [(i, i + 1) for i in range(count - 1)]
        backward = [(target, source) for source, target in forward]
        low = lax.ppermute(
            lax.slice_in_dim(block, block.shape[dim] - width, None, axis=dim), axis, forward
        )
        high = lax.ppermute(lax.slice_in_dim(block, 0, width, axis=dim), axis, backward)
        block = jnp.concatenate([low, block, high], axis=dim)
    return block


def shift_line(values, offset):
    if offset == 0:
        return values
    zeros = jnp.zeros_like(values[:, : abs(offset)])
    if offset > 0:
        return jnp.concatenate([values[:, offset:], zeros], axis=1)
    return jnp.concatenate([zeros, values[:, :offset]], axis=1)


def taps_forward(inputs, weight, spread):
    summed = jnp.zeros(inputs.shape[:3] + (weight.shape[-1],), jnp.float32)
    for shift_tap in range(3):
        shifted = shift_line(inputs, (shift_tap - 1) * spread)
        summed = summed + jnp.einsum(
            "flgi,gio->flgo", shifted, weight[shift_tap], preferred_element_type=jnp.float32
        )
    return summed


def taps_weight_grad(inputs, cotangent, spread, exact):
    pieces = []
    for shift_tap in range(3):
        shifted = shift_line(inputs, (shift_tap - 1) * spread)
        if exact:
            pieces.append(
                jnp.einsum(
                    "flgi,flgo->gio", shifted.astype(jnp.float32), cotangent, precision=highest
                )
            )
        else:
            pieces.append(
                jnp.einsum("flgi,flgo->gio", shifted, cotangent, preferred_element_type=jnp.float32)
            )
    return jnp.stack(pieces)


def taps_input_grad(cotangent, weight, spread):
    summed = jnp.zeros(cotangent.shape[:3] + (weight.shape[2],), jnp.float32)
    for shift_tap in range(3):
        moved = jnp.einsum(
            "flgo,gio->flgi", cotangent, weight[shift_tap], preferred_element_type=jnp.float32
        )
        summed = summed + shift_line(moved, -(shift_tap - 1) * spread)
    return summed


def encoder_forward(sar_faces, first_w, second_w):
    face_count, length, channels_in = sar_faces.shape
    groups = first_w.shape[1]
    inputs = sar_faces.reshape(face_count, length, groups, -1)
    first_out = taps_forward(inputs, first_w, 1)
    hidden = jax.nn.silu(first_out).astype(jnp.bfloat16)
    second = taps_forward(hidden, second_w, 2)
    encoded = (
        (hidden.astype(jnp.float32) + second).reshape(face_count, length, -1).astype(jnp.bfloat16)
    )
    return (encoded, (inputs, first_out, hidden))


def encoder_backward(saved, grad_face, first_w, second_w):
    inputs, first_out, hidden = saved
    groups = first_w.shape[1]
    face_count, length, channels = grad_face.shape
    cotangent = grad_face.reshape(face_count, length, groups, -1)
    second_part = taps_weight_grad(hidden, cotangent, 2, False)
    grad_hidden = cotangent.astype(jnp.float32) + taps_input_grad(cotangent, second_w, 2)
    logistic = jax.nn.sigmoid(first_out)
    grad_first_out = grad_hidden * logistic * (1.0 + first_out * (1.0 - logistic))
    first_part = taps_weight_grad(inputs, grad_first_out, 1, True)
    return (first_part, second_part)


def convolve_forward(padded, kernel, rows, columns):
    channels = kernel.shape[-1]
    summed = jnp.zeros((rows * columns, channels), jnp.float32)
    for row_tap in range(3):
        for col_tap in range(3):
            window = padded[row_tap : row_tap + rows, col_tap : col_tap + columns].reshape(
                -1, channels
            )
            summed = summed + jnp.dot(
                window, kernel[3 * row_tap + col_tap], preferred_element_type=jnp.float32
            )
    return summed


def convolve_backward(padded_act, padded_grad, kernel, rows, columns):
    channels = kernel.shape[-1]
    incoming = padded_grad[1 : rows + 1, 1 : columns + 1].reshape(-1, channels)
    flows = jnp.zeros((rows * columns, channels), jnp.float32)
    kernels = []
    for row_tap in range(3):
        for col_tap in range(3):
            window = padded_act[row_tap : row_tap + rows, col_tap : col_tap + columns].reshape(
                -1, channels
            )
            kernels.append(
                lax.dot_general(
                    window, incoming, (((0,), (0,)), ((), ())), preferred_element_type=jnp.float32
                )
            )
            moved = padded_grad[
                2 - row_tap : 2 - row_tap + rows, 2 - col_tap : 2 - col_tap + columns
            ].reshape(-1, channels)
            flows = flows + lax.dot_general(
                moved,
                kernel[3 * row_tap + col_tap],
                (((1,), (1,)), ((), ())),
                preferred_element_type=jnp.float32,
            )
    return (flows, jnp.stack(kernels))


def norm_backward(flows, lifted, normed, inverse, gain):
    logistic = jax.nn.sigmoid(lifted)
    grad_lift = flows * logistic * (1.0 + lifted * (1.0 - logistic))
    gain_part = jnp.sum(grad_lift * normed, axis=0)
    grad_norm = grad_lift * gain
    grad_hsum = inverse * (
        grad_norm - normed * jnp.mean(grad_norm * normed, axis=-1, keepdims=True)
    )
    return (gain_part, grad_hsum)


MESH = pl.DeviceIdType.MESH
VM = pltpu.VMEM
ANY = pl.ANY
F32 = jnp.float32
BF16 = jnp.bfloat16
ZERO, CROSS = 17, 16
PARTS = 2


class Gather:
    def __init__(self, buf, send, recv):
        self.buf, self.send_sem, self.recv_sem = buf, send, recv
        self.rows = buf.shape[1] // PARTS
        self.me = lax.axis_index("tile")
        self.core = lax.rem(self.me, 2)
        self.x = lax.rem(self.me // 2, 2)
        self.z = z = self.me // 4
        self.x_peer = z * 4 + (1 - self.x) * 2 + self.core
        self.sibling = z * 4 + self.x * 2 + (1 - self.core)
        self.planes = [
            z,
            jnp.where(z == 0, 1, z - 1),
            jnp.where(z == 0, 2, jnp.where(z == 3, 1, z + 1)),
            jnp.where(z < 2, 3, 0),
        ]

    def copy(self, chunk, s, to, index):
        part = self.buf.at[chunk, pl.ds(s * self.rows, self.rows)]
        return pltpu.make_async_remote_copy(
            src_ref=part,
            dst_ref=part,
            send_sem=self.send_sem.at[index * PARTS + s],
            recv_sem=self.recv_sem.at[chunk, s],
            device_id={"tile": to},
            device_id_type=MESH,
        )

    def at(self, step, x, core):
        return self.planes[step] * 4 + x * 2 + core

    def along(self, step):
        onward = jnp.where(self.planes[step] < self.z, self.z + 1, self.z - 1)
        valid = (onward >= 0) & (onward <= 3)
        return jnp.clip(onward, 0, 3) * 4 + lax.rem(self.me, 4), valid

    def start(self, s):
        place = lax.rem(self.me, 4)
        if s:
            self.copy(self.me, s - 1, self.x_peer, 2).wait_send()

        @pl.when(self.z < 3)
        def _():
            self.copy(self.me, s, jnp.minimum(self.z + 1, 3) * 4 + place, 0).start()

        @pl.when(self.z > 0)
        def _():
            self.copy(self.me, s, jnp.maximum(self.z - 1, 0) * 4 + place, 1).start()

        self.copy(self.me, s, self.x_peer, 2).start()
        self.copy(self.me, s, self.sibling, 3).start()

    def pass_z(self, step, s):
        chunk = self.at(step, self.x, self.core)
        self.copy(chunk, s, self.x_peer, 0).wait_recv()
        to, valid = self.along(step)

        @pl.when(valid)
        def _():
            self.copy(chunk, s, to, 3 + step).start()

        self.copy(chunk, s, self.x_peer, 6 + step).start()
        self.copy(chunk, s, self.sibling, 9 + step).start()

    def pass_x(self, step, s):
        chunk = self.at(step, 1 - self.x, self.core)
        self.copy(chunk, s, self.sibling, 0).wait_recv()
        self.copy(chunk, s, self.sibling, 13 + step).start()

    def relay(self, ends, middles=None):
        def run(names):
            for name in names.split():
                step, s = int(name[1]), int(name[2])
                if name[0] == "Z":
                    self.pass_z(step, s)
                else:
                    self.pass_x(step, s)

        if middles is None:
            run(ends)
            return
        middle = (self.z > 0) & (self.z < 3)

        @pl.when(middle)
        def _():
            run(middles)

        @pl.when(jnp.logical_not(middle))
        def _():
            run(ends)

    def take(self, step):
        for x in (self.x, 1 - self.x):
            for s in range(PARTS):
                chunk = self.at(step, x, 1 - self.core)
                self.copy(chunk, s, self.sibling, 0).wait_recv()

    def drain(self):
        for s in range(PARTS):

            @pl.when(self.z < 3)
            def _():
                self.copy(self.me, s, self.sibling, 0).wait_send()

            @pl.when(self.z > 0)
            def _():
                self.copy(self.me, s, self.sibling, 1).wait_send()

            for step in range(1, 4):
                _, valid = self.along(step)

                @pl.when(valid)
                def _():
                    self.copy(self.me, s, self.sibling, 3 + step).wait_send()

            if s == PARTS - 1:
                self.copy(self.me, s, self.sibling, 2).wait_send()
            for index in (3, 7, 8, 9, 10, 11, 12, 13, 14, 15, 16):
                self.copy(self.me, s, self.sibling, index).wait_send()


def moved(values, offset, axis):
    extent = values.shape[axis]
    rolled = pltpu.roll(values, (-offset) % extent, axis)
    place = lax.broadcasted_iota(jnp.int32, values.shape, axis)
    return jnp.where(place == (extent - 1 if offset > 0 else 0), 0.0, rolled)


def iota(shape, axis):
    return lax.broadcasted_iota(jnp.int32, shape, axis)


def over_48(index):
    return ((index >> 4) * 171) >> 9


def along_face(values, offset):
    if offset == 0:
        return values
    rolled = pltpu.roll(values, (-offset) % values.shape[0], 0)
    place = (iota(values.shape, 0) & 7) + offset
    return jnp.where((place >= 0) & (place < 8), rolled, 0.0)


def dot(left, right):
    return jnp.dot(left, right, preferred_element_type=F32)


def dot_back(left, right):
    return lax.dot_general(left, right, (((1,), (1,)), ((), ())), preferred_element_type=F32)


def wide(values):
    return jnp.concatenate([values, values, values], axis=1)


class Crossing:
    def __init__(self, buf, sems):
        me = lax.axis_index("tile")
        place = lax.rem(me, 4)
        self.goes = ((place == 0) & (me > 0)) | ((place == 3) & (me < 15))
        to = jnp.where(place == 0, jnp.maximum(me - 1, 0), jnp.minimum(me + 1, 15))
        self.copy = pltpu.make_async_remote_copy(
            src_ref=buf.at[me],
            dst_ref=buf.at[CROSS],
            send_sem=sems.at[0],
            recv_sem=sems.at[1],
            device_id={"tile": to},
            device_id_type=MESH,
        )
        self.above = jnp.where(place > 0, me - 1, jnp.where(me > 0, CROSS, ZERO))
        self.below = jnp.where(place < 3, me + 1, jnp.where(me < 15, CROSS, ZERO))

    def start(self):
        @pl.when(self.goes)
        def _():
            self.copy.start()

    def wait_recv(self):
        @pl.when(self.goes)
        def _():
            self.copy.wait_recv()

    def wait_send(self):
        @pl.when(self.goes)
        def _():
            self.copy.wait_send()


def step_kernel(
    time_ref,
    owner_hbm,
    slot_hbm,
    count_hbm,
    faces_hbm,
    mask_hbm,
    gain_hbm,
    w1_hbm,
    w2_hbm,
    clean_hbm,
    noise_hbm,
    kernel_hbm,
    acc_ref,
    shifted,
    gbuf,
    small_ref,
    owner_ref,
    slot_ref,
    count_ref,
    faces_ref,
    mask_ref,
    gain_ref,
    w1_ref,
    w2_ref,
    clean_ref,
    noise_ref,
    kernel_ref,
    load_sems,
    sbuf,
    rbuf,
    x_send,
    x_recv,
    w1_dense,
    w2_dense,
    mixed,
    first_out,
    inputs,
    hiddens,
    chosen,
    inv_cov,
    inverse_ref,
    normed_ref,
    act_ref,
    abuf,
    a_send,
    a_recv,
    g_send,
    g_recv,
    g_cross,
    small_out,
    small_in,
    s_send,
    s_recv,
    t_send,
    t_recv,
    half_send,
    half_recv,
):
    me = lax.axis_index("tile")
    barrier = pltpu.get_barrier_semaphore()
    for k in range(1, 16):
        pl.semaphore_signal(
            barrier, inc=1, device_id={"tile": lax.rem(me + k, 16)}, device_id_type=MESH
        )
    pairs = (
        (owner_hbm, owner_ref),
        (slot_hbm, slot_ref),
        (count_hbm, count_ref),
        (faces_hbm, faces_ref),
        (mask_hbm, mask_ref),
        (gain_hbm, gain_ref),
        (w1_hbm, w1_ref),
        (w2_hbm, w2_ref),
        (clean_hbm, clean_ref),
        (noise_hbm, noise_ref),
        (kernel_hbm, kernel_ref),
    )
    loads = [
        pltpu.make_async_copy(far, near, load_sems.at[i]) for i, (far, near) in enumerate(pairs)
    ]
    for load in loads:
        load.start()
    core = lax.rem(me, 2)
    pixels, channels = act_ref.shape
    faces = owner_ref.shape[1]

    for load in loads[:4]:
        load.wait()
    square = (faces, faces)
    diagonal = iota(square, 0) == iota(square, 1)
    owner_row = owner_ref[...].astype(F32)
    owner_col = jnp.sum(jnp.where(diagonal, owner_row, 0.0), axis=1, keepdims=True)
    earlier = (owner_col == owner_row) & (iota(square, 1) < iota(square, 0))
    within = jnp.sum(jnp.where(earlier, 1.0, 0.0), axis=1, keepdims=True)
    goes_to = owner_col * 16.0 + within * 8.0
    lines = 8 * faces
    of_face = iota((faces, lines), 0) == (iota((faces, lines), 1) >> 3)
    row_of = jnp.sum(jnp.where(of_face, goes_to, 0.0), axis=0, keepdims=True)
    row_of = row_of + (iota((1, lines), 1) & 7).astype(F32)
    packer = jnp.where(iota((256, lines), 0).astype(F32) == row_of, 1.0, 0.0).astype(BF16)
    mine = (iota((lines, faces), 0) >> 3) == iota((lines, faces), 1)
    slot_of = jnp.sum(
        jnp.where(mine, slot_ref[...].astype(F32), 0.0), axis=1, keepdims=True
    )
    count_of = jnp.sum(
        jnp.where(mine, count_ref[...].astype(F32), 0.0), axis=1, keepdims=True
    )
    pixel = (iota((lines, 1), 0) & 7).astype(F32)
    label = jnp.where(pixel < count_of, slot_of * 8.0 + pixel + 1.0, 0.0)
    sbuf[:, 0:16, :] = dot(packer, faces_ref[...]).astype(BF16).reshape(16, 16, 128)
    sbuf[:, 16:32, :] = (
        dot(packer, jnp.broadcast_to(label, (lines, 128)).astype(BF16))
        .astype(BF16)
        .reshape(16, 16, 128)
    )
    pl.semaphore_wait(barrier, 15)
    sends = []
    for k in range(1, 16):
        to = lax.rem(me + k, 16)
        send = pltpu.make_async_remote_copy(
            src_ref=sbuf.at[to],
            dst_ref=rbuf.at[me],
            send_sem=x_send.at[k - 1],
            recv_sem=x_recv.at[k - 1],
            device_id={"tile": to},
            device_id_type=MESH,
        )
        send.start()
        sends.append(send)
    rbuf[me] = sbuf[me]
    for load in loads[4:]:
        load.wait()
    spread = (
        iota((48, channels), 1) - 48 * over_48(iota((48, channels), 1)) == iota((48, channels), 0)
    )
    spread = jnp.where(spread, 1.0, 0.0).astype(BF16)
    group_of = over_48(iota((1, channels), 1))
    keep1 = (iota((128, 1), 0) >> 4) == group_of
    keep2 = over_48(iota((channels, 1), 0)) == group_of
    for k in range(3):
        dense = dot(w1_ref[k * 128 : (k + 1) * 128], spread)
        w1_dense[k] = jnp.where(keep1, dense, 0.0).astype(BF16)
        dense = dot(w2_ref[k * channels : (k + 1) * channels], spread)
        w2_dense[k] = jnp.where(keep2, dense, 0.0).astype(BF16)
    time_value = (jnp.full((1, channels), time_ref[0], jnp.int32).astype(F32) + 0.5) / NSTEPS
    mixed[...] = (1.0 - time_value) * noise_ref[...].astype(F32) + time_value * clean_ref[
        ...
    ].astype(F32)
    on_diagonal = iota((pixels, pixels), 0) == iota((pixels, pixels), 1)
    cloudy = jnp.where(on_diagonal, mask_ref[...].astype(F32), 0.0).astype(BF16)
    pixel_weight = (1.0 + dot(cloudy, jnp.ones((pixels, 128), BF16))) / pixels
    zero_pixels = jnp.zeros((3 * channels, pixels), BF16)
    shifted[:, 0:pixels] = zero_pixels
    shifted[:, 17 * pixels : 18 * pixels] = zero_pixels
    abuf[ZERO] = jnp.zeros((channels, pixels), BF16)
    gbuf[ZERO] = jnp.zeros((pixels, channels), BF16)
    for send in sends:
        send.wait()
    plain = rbuf[:, 0:16, :].reshape(256, 128).astype(F32)
    total = jnp.zeros((256, channels), F32)
    for k in range(3):
        inputs[k] = along_face(plain, k - 1).astype(BF16)
        total = total + dot(inputs[k], w1_dense[k])
    first_out[...] = total
    hidden = (total * jax.nn.sigmoid(total)).astype(BF16)
    hidden_wide = hidden.astype(F32)
    total = hidden_wide
    for k in range(3):
        hiddens[k] = along_face(hidden_wide, 2 * (k - 1)).astype(BF16)
        total = total + dot(hiddens[k], w2_dense[k])
    encoded = total.astype(BF16)
    labels = rbuf[:, 16:32, :].reshape(256, 128).astype(F32)
    hits = jnp.concatenate([labels, labels], axis=1) == (iota((256, pixels), 1) + 1).astype(F32)
    chosen[...] = jnp.where(hits, 1.0, 0.0).astype(BF16)
    placer = chosen[...].T
    inv_cov[...] = 1.0 / (1.0 + dot(placer, jnp.ones((256, 128), BF16)))
    hsum = mixed[...] + dot(placer, encoded) * wide(inv_cov[...])
    inverse = lax.rsqrt(jnp.mean(hsum * hsum, axis=1, keepdims=True) + epsilon)
    inverse_ref[...] = jnp.broadcast_to(inverse, (pixels, 128))
    normed_ref[...] = hsum * inverse
    lifted = normed_ref[...] * gain_ref[...].reshape(1, channels)
    act_ref[...] = (lifted * jax.nn.sigmoid(lifted)).astype(BF16)
    abuf[me] = act_ref[...].T
    acts = Gather(abuf, a_send, a_recv)
    acts.start(0)
    own = act_ref[...]
    sums = [dot(own, kernel_ref[3 + d]) for d in range(3)]
    acts.start(1)
    part = channels // 2
    half = pl.ds(pl.multiple_of(core * part, part), part)

    def shift_one(chunk):
        plain = abuf[chunk]
        values = plain.astype(F32)
        here = pl.ds(pl.multiple_of((chunk + 1) * pixels, pixels), pixels)
        shifted[0:channels, here] = moved(values, -1, 1).astype(BF16)
        shifted[channels : 2 * channels, here] = plain
        shifted[2 * channels : 3 * channels, here] = moved(values, 1, 1).astype(BF16)

    def shift_plane(order):
        base = acts.planes[order] * 4

        def step(i, carry):
            shift_one(base + i)
            return carry

        lax.fori_loop(0, 4, step, 0)

    def half_copy(row):
        return pltpu.make_async_remote_copy(
            src_ref=acc_ref.at[pl.ds(3 * row, 3), half],
            dst_ref=acc_ref.at[pl.ds(3 * row, 3), half],
            send_sem=half_send.at[row],
            recv_sem=half_recv.at[row],
            device_id={"tile": acts.sibling},
            device_id_type=MESH,
        )

    def multiply(order, row):
        base = acts.planes[order] * 4
        right = gbuf[pl.ds(base, 4)].reshape(4 * pixels, channels)
        start = pl.multiple_of((base + row) * pixels, pixels)
        for d in range(3):
            rows = pl.ds(pl.multiple_of(d * channels + core * part, part), part)
            piece = dot(shifted[rows, pl.ds(start, 4 * pixels)], right)
            if order == 0:
                acc_ref[3 * row + d, half, :] = piece
            else:
                acc_ref[3 * row + d, half, :] = acc_ref[3 * row + d, half, :] + piece
        if order == 2:
            half_copy(row).start()

    acts.relay("X00 Z10 X01 Z11", "X00 Z10 Z20 X01 Z11 Z21")
    acts.take(0)
    shift_plane(0)
    acts.relay("Z20 X10 Z21 X11", "Z30 X10 X20 Z31 X11 X21")
    acts.take(1)
    acts.relay("Z30 X20 Z31 X21", "")
    acts.take(2)
    above = abuf[jnp.where(me > 0, me - 1, ZERO)].T
    below = abuf[jnp.where(me < 15, me + 1, ZERO)].T
    sums = [
        sums[d] + dot(above, kernel_ref[d]) + dot(below, kernel_ref[6 + d]) for d in range(3)
    ]
    predicted = sums[1] + moved(sums[0], -1, 0) + moved(sums[2], 1, 0)
    grad = (
        wide(pixel_weight)
        * (predicted - clean_ref[...].astype(F32) + noise_ref[...].astype(F32))
    ).astype(BF16)
    gbuf[me] = grad
    grads = Gather(gbuf, g_send, g_recv)
    g_row = Crossing(gbuf, g_cross)
    g_row.start()
    grads.start(0)
    own = gbuf[me]
    sums = [dot_back(own, kernel_ref[3 + d]) for d in range(3)]
    acts.relay("X30 X31")
    grads.start(1)
    shift_plane(1)
    shift_plane(2)
    grads.relay("X00 Z10 X01 Z11", "X00 Z10 Z20 X01 Z11 Z21")
    grads.take(0)
    acts.take(3)
    g_row.wait_recv()
    above = gbuf[g_row.above]
    below = gbuf[g_row.below]
    sums = [
        sums[d] + dot_back(below, kernel_ref[d]) + dot_back(above, kernel_ref[6 + d])
        for d in range(3)
    ]
    flows = sums[1] + moved(sums[0], 1, 0) + moved(sums[2], -1, 0)

    gain = gain_ref[...].reshape(1, channels)
    normed = normed_ref[...]
    lifted = normed * gain
    logistic = jax.nn.sigmoid(lifted)
    grad_lift = flows * logistic * (1.0 + lifted * (1.0 - logistic))
    gain_part = jnp.sum(grad_lift * normed, axis=0, keepdims=True)
    grad_norm = grad_lift * gain
    grad_hsum = wide(inverse_ref[...]) * (
        grad_norm - normed * jnp.mean(grad_norm * normed, axis=1, keepdims=True)
    )
    scaled = (grad_hsum * wide(inv_cov[...])).astype(BF16)
    grads.relay("Z20 X10", "Z30")
    cotangent_wide = dot(chosen[...], scaled)
    cotangent = cotangent_wide.astype(BF16)
    grad_hidden = cotangent_wide
    small_rows = []
    for k in range(3):
        grad_hidden = grad_hidden + dot_back(
            along_face(cotangent_wide, -2 * (k - 1)).astype(BF16), w2_dense[k]
        )
        product = jnp.where(keep2, dot(hiddens[k].T, cotangent), 0.0)
        small_rows.append(sum(product[48 * g : 48 * (g + 1)] for g in range(8)))
    logistic = jax.nn.sigmoid(first_out[...])
    grad_first = grad_hidden * logistic * (1.0 + first_out[...] * (1.0 - logistic))
    grad_high = grad_first.astype(BF16)
    grad_low = (grad_first - grad_high.astype(F32)).astype(BF16)
    for k in range(3):
        turned = inputs[k].T
        product = jnp.where(keep1, dot(turned, grad_high) + dot(turned, grad_low), 0.0)
        small_rows.append(sum(product[16 * g : 16 * (g + 1)] for g in range(8)))
    small_rows.append(
        jnp.where(iota((16, channels), 0) == 0, jnp.broadcast_to(gain_part, (16, channels)), 0.0)
    )
    small_out[...] = jnp.concatenate(small_rows, axis=0).astype(BF16)
    def small_send(k):
        to = lax.rem(me + k, 16)
        rows = pl.ds(pl.multiple_of(jnp.minimum(to, 12) * 16, 16), 16)
        return to < 13, pltpu.make_async_remote_copy(
            src_ref=small_out.at[rows],
            dst_ref=small_in.at[me],
            send_sem=s_send.at[k - 1],
            recv_sem=s_recv.at[k - 1],
            device_id={"tile": to},
            device_id_type=MESH,
        )

    my_rows = pl.ds(pl.multiple_of(jnp.minimum(me, 12) * 16, 16), 16)

    def small_spread(k):
        return pltpu.make_async_remote_copy(
            src_ref=small_ref.at[my_rows],
            dst_ref=small_ref.at[my_rows],
            send_sem=t_send.at[k - 1],
            recv_sem=t_recv.at[k - 1],
            device_id={"tile": lax.rem(me + k, 16)},
            device_id_type=MESH,
        )

    for k in range(1, 16):
        valid, send = small_send(k)

        @pl.when(valid)
        def _():
            send.start()

    grads.relay("Z21 X11", "X10 X20 Z31")
    multiply(0, 0)
    grads.relay("Z30 X20", "X11 X21")
    multiply(0, 1)
    shift_plane(3)
    grads.relay("Z31", "")
    multiply(0, 2)
    grads.relay("X21", "")
    grads.take(1)
    multiply(1, 0)

    @pl.when(me < 13)
    def _():
        for k in range(1, 16):
            small_send(k)[1].wait_recv()
        small_in[me] = small_out[my_rows, :]
        added = small_in[0].astype(F32)
        for k in range(1, 16):
            added = added + small_in[k].astype(F32)
        small_ref[my_rows, :] = added.astype(BF16)
        for k in range(1, 16):
            small_spread(k).start()

    grads.relay("X30")
    multiply(1, 1)
    multiply(1, 2)
    grads.take(2)
    multiply(2, 0)
    grads.relay("X31")
    multiply(2, 1)
    multiply(2, 2)
    for k in range(1, 16):

        @pl.when(lax.rem(me + 16 - k, 16) < 13)
        def _():
            small_spread(k).wait_recv()

    grads.take(3)
    for row in range(3):
        half_copy(row).wait()

    @pl.when(me < 13)
    def _():
        for k in range(1, 16):
            small_spread(k).wait_send()

    for k in range(1, 16):
        valid, send = small_send(k)

        @pl.when(valid)
        def _():
            send.wait_send()

    acts.drain()
    grads.drain()
    g_row.wait_send()


def step_call(
    time_index, owner, slot, count, faces, mask, gain, first_w, second_w, clean, noise, kernel
):
    pixels, channels = clean.shape
    dma = pltpu.SemaphoreType.DMA
    whole = pl.BlockSpec(memory_space=VM)
    staged = (owner, slot, count, faces, mask, gain, first_w, second_w, clean, noise, kernel)
    staged = tuple(pltpu.with_memory_space_constraint(array, pltpu.HBM) for array in staged)
    return pl.pallas_call(
        step_kernel,
        out_shape=(
            jax.ShapeDtypeStruct((9, channels, channels), F32),
            jax.ShapeDtypeStruct((3 * channels, 18 * pixels), BF16),
            jax.ShapeDtypeStruct((18, pixels, channels), BF16),
            jax.ShapeDtypeStruct((208, channels), BF16),
        ),
        in_specs=[pl.BlockSpec(memory_space=pltpu.SMEM)]
        + [pl.BlockSpec(memory_space=ANY)] * len(staged),
        out_specs=(whole,) * 4,
        scratch_shapes=[VM(array.shape, array.dtype) for array in staged]
        + [
            dma((len(staged),)),
            VM((16, 32, 128), BF16),
            VM((16, 32, 128), BF16),
            dma((15,)),
            dma((15,)),
            VM((3, 128, channels), BF16),
            VM((3, channels, channels), BF16),
            VM((pixels, channels), F32),
            VM((256, channels), F32),
            VM((3, 256, 128), BF16),
            VM((3, 256, channels), BF16),
            VM((256, pixels), BF16),
            VM((pixels, 128), F32),
            VM((pixels, 128), F32),
            VM((pixels, channels), F32),
            VM((pixels, channels), BF16),
            VM((18, channels, pixels), BF16),
            dma((17 * PARTS,)),
            dma((16, PARTS)),
            dma((17 * PARTS,)),
            dma((16, PARTS)),
            dma((2,)),
            VM((208, channels), BF16),
            VM((16, 16, channels), BF16),
            dma((15,)),
            dma((15,)),
            dma((15,)),
            dma((15,)),
            dma((3,)),
            dma((3,)),
        ],
        compiler_params=pltpu.CompilerParams(
            collective_id=0, has_side_effects=True, vmem_limit_bytes=28 * 2**20
        ),
        name="step",
    )(time_index, *staged)


def finish_kernel(
    acc_ref, shifted, gbuf, small_ref, kernel_out, gain_out, first_out, second_out, held, sems
):
    me = lax.axis_index("tile")
    channels = acc_ref.shape[1]
    pixels = gbuf.shape[1]
    z = me // 4
    base = 4 * jnp.where(z < 2, 3, 0)
    right = gbuf[pl.ds(base, 4)].reshape(4 * pixels, channels)

    def step(row, carry):
        start = pl.multiple_of((base + row) * pixels, pixels)
        for d in range(3):
            tap = 3 * row + d
            left = shifted[d * channels : (d + 1) * channels, pl.ds(start, 4 * pixels)]
            held[tap] = acc_ref[tap] + dot(left, right)
            pltpu.make_async_copy(held.at[tap], kernel_out.at[tap], sems.at[tap]).start()
        return carry

    lax.fori_loop(0, 3, step, 0)
    summed = small_ref[...].astype(F32)
    for k in range(3):
        second = summed[48 * k : 48 * (k + 1)]
        first = summed[144 + 16 * k : 144 + 16 * (k + 1)]
        for g in range(8):
            turn = (channels - 48 * g) % channels
            turned = pltpu.roll(second, turn, 1)[:, :48] if turn else second[:, :48]
            second_out[(8 * k + g) * 48 : (8 * k + g + 1) * 48, :] = turned
            turned = pltpu.roll(first, turn, 1)[:, :48] if turn else first[:, :48]
            first_out[(8 * k + g) * 16 : (8 * k + g + 1) * 16, :] = turned
    gain_out[...] = summed[192]
    for tap in range(9):
        pltpu.make_async_copy(held.at[tap], kernel_out.at[tap], sems.at[tap]).wait()


def finish_call(acc, shifted, grads, small):
    channels = acc.shape[1]
    whole = pl.BlockSpec(memory_space=VM)
    return pl.pallas_call(
        finish_kernel,
        out_shape=(
            jax.ShapeDtypeStruct(acc.shape, F32),
            jax.ShapeDtypeStruct((channels,), F32),
            jax.ShapeDtypeStruct((384, 48), F32),
            jax.ShapeDtypeStruct((1152, 48), F32),
        ),
        in_specs=[whole] * 4,
        out_specs=(pl.BlockSpec(memory_space=ANY), whole, whole, whole),
        scratch_shapes=[VM(acc.shape, F32), pltpu.SemaphoreType.DMA((9,))],
        compiler_params=pltpu.CompilerParams(vmem_limit_bytes=12 * 2**20),
        name="finish",
    )(acc, shifted, grads, small)


def body16(
    sar_faces,
    dest_owner,
    face_slot,
    valid_pixels,
    cloud_mask,
    time_index,
    clean_latent,
    noise_latent,
    encoder_first,
    encoder_second,
    conv_kernel,
    norm_gain,
):
    channels_in = sar_faces.shape[-1]
    channels = clean_latent.shape[-1]
    acc, shifted, grads, small = step_call(
        time_index,
        dest_owner.reshape(1, -1),
        face_slot.reshape(1, -1),
        valid_pixels.reshape(1, -1),
        sar_faces.reshape(-1, channels_in),
        cloud_mask,
        norm_gain,
        encoder_first.reshape(-1, encoder_first.shape[-1]),
        encoder_second.reshape(-1, encoder_second.shape[-1]),
        clean_latent.reshape(-1, channels),
        noise_latent.reshape(-1, channels),
        conv_kernel,
    )
    grad_kernel, grad_gain, grad_first, grad_second = finish_call(acc, shifted, grads, small)
    return (
        grad_kernel,
        grad_gain,
        grad_first.reshape(encoder_first.shape),
        grad_second.reshape(encoder_second.shape),
    )


def body(
    sar_faces,
    dest_owner,
    face_slot,
    valid_pixels,
    cloud_mask,
    time_index,
    clean_latent,
    noise_latent,
    encoder_first,
    encoder_second,
    conv_kernel,
    norm_gain,
):
    owners = lax.axis_size("tile")
    slot_total = owners * MOST
    face_count, length, channels_in = sar_faces.shape
    rows, columns, channels = clean_latent.shape
    tile_faces = rows * columns // length
    owner_list = dest_owner[:, 0]
    order = jnp.arange(face_count, dtype=jnp.int32)
    within = jnp.sum(
        (
            (owner_list[:, None] == owner_list[None, :]) & (order[None, :] < order[:, None])
        ).astype(jnp.int32),
        axis=1,
    )
    buffer_at = owner_list * MOST + within
    placed = (jnp.arange(slot_total, dtype=jnp.int32)[:, None] == buffer_at[None, :]).astype(
        jnp.int32
    )
    placer = placed.astype(jnp.bfloat16)
    labels = jnp.stack(
        [
            jnp.sum(placed * face_slot[None, :], axis=1),
            jnp.sum(placed * valid_pixels[None, :], axis=1),
        ],
        axis=-1,
    )
    labels = labels.reshape(owners, MOST, 2)
    packed = jnp.einsum(
        "sf,fjc->sjc", placer, sar_faces, preferred_element_type=jnp.float32
    ).astype(jnp.bfloat16)
    arrived, recv_labels = (
        lax.all_to_all(
            packed.reshape(owners, MOST, length, channels_in),
            "tile",
            split_axis=0,
            concat_axis=0,
            tiled=True,
        ),
        lax.all_to_all(labels, "tile", split_axis=0, concat_axis=0, tiled=True),
    )
    raw_slots = arrived.reshape(slot_total, length, channels_in)
    received, saved = encoder_forward(raw_slots, encoder_first, encoder_second)
    recv_labels = recv_labels.reshape(slot_total, 2)
    recv_slot = recv_labels[:, 0]
    recv_count = recv_labels[:, 1]
    validity = (jnp.arange(length, dtype=jnp.int32)[None, :] < recv_count[:, None]).astype(
        jnp.float32
    )
    selector = recv_slot[:, None] == jnp.arange(tile_faces, dtype=jnp.int32)[None, :]
    masked = received * validity[..., None].astype(jnp.bfloat16)
    summed = jnp.einsum(
        "sp,sjc->pjc", selector.astype(jnp.bfloat16), masked, preferred_element_type=jnp.float32
    )
    covered = jnp.einsum(
        "sp,sj->pj", selector.astype(jnp.float32), validity, precision=highest
    ).reshape(-1, 1)
    condition = summed.reshape(-1, channels) / (1.0 + covered)
    time_value = (time_index[0].astype(jnp.float32) + 0.5) / NSTEPS
    noise_flat = noise_latent.astype(jnp.float32).reshape(-1, channels)
    clean_flat = clean_latent.astype(jnp.float32).reshape(-1, channels)
    hsum = (1.0 - time_value) * noise_flat + time_value * clean_flat + condition
    inverse = lax.rsqrt(jnp.mean(hsum * hsum, axis=-1, keepdims=True) + epsilon)
    normed = hsum * inverse
    lifted = normed * norm_gain
    activated = jax.nn.silu(lifted).astype(jnp.bfloat16).reshape(rows, columns, channels)
    extended = with_halo(activated, (("tile", 0),), 1)
    padded = jnp.pad(extended, ((0, 0), (1, 1), (0, 0)))
    predicted = convolve_forward(padded, conv_kernel, rows, columns)
    pixel_weight = (1 + cloud_mask).astype(jnp.float32).reshape(-1, 1)
    grad_pred = (pixel_weight * (predicted - clean_flat + noise_flat) / (rows * columns)).astype(
        jnp.bfloat16
    )
    grad_rows = with_halo(grad_pred.reshape(rows, columns, channels), (("tile", 0),), 1)
    padded_grad = jnp.pad(grad_rows, ((0, 0), (1, 1), (0, 0)))
    flows, kernel_part = convolve_backward(padded, padded_grad, conv_kernel, rows, columns)
    gain_part, grad_hsum = norm_backward(flows, lifted, normed, inverse, norm_gain)
    scaled = (grad_hsum / (1.0 + covered)).astype(jnp.bfloat16)
    target = recv_slot[:, None] * length + jnp.arange(length, dtype=jnp.int32)[None, :]
    target = jnp.where(validity > 0, target, -1).reshape(-1)
    picker = target[:, None] == jnp.arange(rows * columns, dtype=jnp.int32)[None, :]
    slot_grads = jnp.dot(
        picker.astype(jnp.bfloat16), scaled, preferred_element_type=jnp.float32
    ).astype(jnp.bfloat16)
    slot_grads = slot_grads.reshape(slot_total, length, channels)
    first_part, second_part = encoder_backward(saved, slot_grads, encoder_first, encoder_second)
    reduced = lax.psum((kernel_part, gain_part, first_part, second_part), "tile")
    return (reduced[0], reduced[1], reduced[2], reduced[3])


def solution(mesh):
    placed = (
        P(("groups", "tile"), None, None),
        P(("groups", "tile"), None),
        P(("groups", "tile")),
        P(("groups", "tile")),
        P(("groups", "tile"), None),
        P(("groups", "tile")),
        P(("groups", "tile"), None, None),
        P(("groups", "tile"), None, None),
        P(),
        P(),
        P(),
        P(),
    )
    return jax.shard_map(
        body16 if mesh.shape["tile"] == 16 else body,
        mesh=mesh,
        in_specs=placed,
        out_specs=(
            P("groups", None, None),
            P("groups"),
            P("groups", None, None, None),
            P("groups", None, None, None),
        ),
        check_vma=False,
    )
```

```python
import jax
import jax.numpy as jnp
from jax import lax
from jax.experimental import pallas as pl
from jax.experimental.pallas import tpu as pltpu
from jax.sharding import PartitionSpec as P

MOST = 2
NSTEPS = 1000


highest = lax.Precision.HIGHEST
epsilon = 1e-06


def with_halo(block, sides, width):
    for axis, dim in sides:
        count = lax.axis_size(axis)
        forward = [(i, i + 1) for i in range(count - 1)]
        backward = [(target, source) for source, target in forward]
        low = lax.ppermute(
            lax.slice_in_dim(block, block.shape[dim] - width, None, axis=dim), axis, forward
        )
        high = lax.ppermute(lax.slice_in_dim(block, 0, width, axis=dim), axis, backward)
        block = jnp.concatenate([low, block, high], axis=dim)
    return block


def shift_line(values, offset):
    if offset == 0:
        return values
    zeros = jnp.zeros_like(values[:, : abs(offset)])
    if offset > 0:
        return jnp.concatenate([values[:, offset:], zeros], axis=1)
    return jnp.concatenate([zeros, values[:, :offset]], axis=1)


def taps_forward(inputs, weight, spread):
    summed = jnp.zeros(inputs.shape[:3] + (weight.shape[-1],), jnp.float32)
    for shift_tap in range(3):
        shifted = shift_line(inputs, (shift_tap - 1) * spread)
        summed = summed + jnp.einsum(
            "flgi,gio->flgo", shifted, weight[shift_tap], preferred_element_type=jnp.float32
        )
    return summed


def taps_weight_grad(inputs, cotangent, spread, exact):
    pieces = []
    for shift_tap in range(3):
        shifted = shift_line(inputs, (shift_tap - 1) * spread)
        if exact:
            pieces.append(
                jnp.einsum(
                    "flgi,flgo->gio", shifted.astype(jnp.float32), cotangent, precision=highest
                )
            )
        else:
            pieces.append(
                jnp.einsum("flgi,flgo->gio", shifted, cotangent, preferred_element_type=jnp.float32)
            )
    return jnp.stack(pieces)


def taps_input_grad(cotangent, weight, spread):
    summed = jnp.zeros(cotangent.shape[:3] + (weight.shape[2],), jnp.float32)
    for shift_tap in range(3):
        moved = jnp.einsum(
            "flgo,gio->flgi", cotangent, weight[shift_tap], preferred_element_type=jnp.float32
        )
        summed = summed + shift_line(moved, -(shift_tap - 1) * spread)
    return summed


def encoder_forward(sar_faces, first_w, second_w):
    face_count, length, channels_in = sar_faces.shape
    groups = first_w.shape[1]
    inputs = sar_faces.reshape(face_count, length, groups, -1)
    first_out = taps_forward(inputs, first_w, 1)
    hidden = jax.nn.silu(first_out).astype(jnp.bfloat16)
    second = taps_forward(hidden, second_w, 2)
    encoded = (
        (hidden.astype(jnp.float32) + second).reshape(face_count, length, -1).astype(jnp.bfloat16)
    )
    return (encoded, (inputs, first_out, hidden))


def encoder_backward(saved, grad_face, first_w, second_w):
    inputs, first_out, hidden = saved
    groups = first_w.shape[1]
    face_count, length, channels = grad_face.shape
    cotangent = grad_face.reshape(face_count, length, groups, -1)
    second_part = taps_weight_grad(hidden, cotangent, 2, False)
    grad_hidden = cotangent.astype(jnp.float32) + taps_input_grad(cotangent, second_w, 2)
    logistic = jax.nn.sigmoid(first_out)
    grad_first_out = grad_hidden * logistic * (1.0 + first_out * (1.0 - logistic))
    first_part = taps_weight_grad(inputs, grad_first_out, 1, True)
    return (first_part, second_part)


def convolve_forward(padded, kernel, rows, columns):
    channels = kernel.shape[-1]
    summed = jnp.zeros((rows * columns, channels), jnp.float32)
    for row_tap in range(3):
        for col_tap in range(3):
            window = padded[row_tap : row_tap + rows, col_tap : col_tap + columns].reshape(
                -1, channels
            )
            summed = summed + jnp.dot(
                window, kernel[3 * row_tap + col_tap], preferred_element_type=jnp.float32
            )
    return summed


def convolve_backward(padded_act, padded_grad, kernel, rows, columns):
    channels = kernel.shape[-1]
    incoming = padded_grad[1 : rows + 1, 1 : columns + 1].reshape(-1, channels)
    flows = jnp.zeros((rows * columns, channels), jnp.float32)
    kernels = []
    for row_tap in range(3):
        for col_tap in range(3):
            window = padded_act[row_tap : row_tap + rows, col_tap : col_tap + columns].reshape(
                -1, channels
            )
            kernels.append(
                lax.dot_general(
                    window, incoming, (((0,), (0,)), ((), ())), preferred_element_type=jnp.float32
                )
            )
            moved = padded_grad[
                2 - row_tap : 2 - row_tap + rows, 2 - col_tap : 2 - col_tap + columns
            ].reshape(-1, channels)
            flows = flows + lax.dot_general(
                moved,
                kernel[3 * row_tap + col_tap],
                (((1,), (1,)), ((), ())),
                preferred_element_type=jnp.float32,
            )
    return (flows, jnp.stack(kernels))


def norm_backward(flows, lifted, normed, inverse, gain):
    logistic = jax.nn.sigmoid(lifted)
    grad_lift = flows * logistic * (1.0 + lifted * (1.0 - logistic))
    gain_part = jnp.sum(grad_lift * normed, axis=0)
    grad_norm = grad_lift * gain
    grad_hsum = inverse * (
        grad_norm - normed * jnp.mean(grad_norm * normed, axis=-1, keepdims=True)
    )
    return (gain_part, grad_hsum)


MESH = pl.DeviceIdType.MESH
VM = pltpu.VMEM
ANY = pl.ANY
F32 = jnp.float32
BF16 = jnp.bfloat16
ZERO = 16
PARTS = 2


class Gather:
    def __init__(self, buf, send, recv, paced=True):
        self.paced = paced
        self.buf, self.send_sem, self.recv_sem = buf, send, recv
        self.rows = buf.shape[1] // PARTS
        self.me = lax.axis_index("tile")
        self.core = lax.rem(self.me, 2)
        self.x = lax.rem(self.me // 2, 2)
        self.z = z = self.me // 4
        self.x_peer = z * 4 + (1 - self.x) * 2 + self.core
        self.sibling = z * 4 + self.x * 2 + (1 - self.core)
        self.planes = [
            z,
            jnp.where(z == 0, 1, z - 1),
            jnp.where(z == 0, 2, jnp.where(z == 3, 1, z + 1)),
            jnp.where(z < 2, 3, 0),
        ]
        place = lax.rem(self.me, 4)
        self.crosses = ((place == 0) & (z > 0)) | ((place == 3) & (z < 3))
        self.partner = jnp.where(place == 0, jnp.maximum(self.me - 1, 0), jnp.minimum(self.me + 1, 15))

    def direct_from(self, step):
        plane = self.planes[step]
        return ((plane == self.z + 1) & (self.x == 0) & (self.core == 0)) | (
            (plane == self.z - 1) & (self.x == 1) & (self.core == 1)
        )

    def direct_to(self, step):
        plane = self.planes[step]
        return ((plane == self.z + 1) & (self.x == 1) & (self.core == 0)) | (
            (plane == self.z - 1) & (self.x == 0) & (self.core == 1)
        )

    def cross(self):
        @pl.when(self.crosses)
        def _():
            for s in range(PARTS):
                self.copy(self.me, s, self.partner, 17).start()

    def take_cross(self):
        @pl.when(self.crosses)
        def _():
            for s in range(PARTS):
                self.copy(self.partner, s, self.sibling, 18).wait_recv()
                self.copy(self.partner, s, self.sibling, 18).start()

    def copy(self, chunk, s, to, index):
        part = self.buf.at[chunk, pl.ds(s * self.rows, self.rows)]
        return pltpu.make_async_remote_copy(
            src_ref=part,
            dst_ref=part,
            send_sem=self.send_sem.at[index * PARTS + s],
            recv_sem=self.recv_sem.at[chunk, s],
            device_id={"tile": to},
            device_id_type=MESH,
        )

    def at(self, step, x, core):
        return self.planes[step] * 4 + x * 2 + core

    def along(self, step):
        onward = jnp.where(self.planes[step] < self.z, self.z + 1, self.z - 1)
        valid = (onward >= 0) & (onward <= 3)
        return jnp.clip(onward, 0, 3) * 4 + lax.rem(self.me, 4), valid

    def start(self, s):
        place = lax.rem(self.me, 4)
        if s and self.paced:
            self.copy(self.me, s - 1, self.x_peer, 2).wait_send()

        @pl.when(self.z < 3)
        def _():
            self.copy(self.me, s, jnp.minimum(self.z + 1, 3) * 4 + place, 0).start()

        @pl.when(self.z > 0)
        def _():
            self.copy(self.me, s, jnp.maximum(self.z - 1, 0) * 4 + place, 1).start()

        self.copy(self.me, s, self.x_peer, 2).start()
        self.copy(self.me, s, self.sibling, 3).start()

    def pass_z(self, step, s):
        chunk = self.at(step, self.x, self.core)
        self.copy(chunk, s, self.x_peer, 0).wait_recv()
        to, valid = self.along(step)

        @pl.when(valid)
        def _():
            self.copy(chunk, s, to, 3 + step).start()

        @pl.when(jnp.logical_not(self.direct_from(step)))
        def _():
            self.copy(chunk, s, self.x_peer, 6 + step).start()

        self.copy(chunk, s, self.sibling, 9 + step).start()

    def pass_x(self, step, s):
        chunk = self.at(step, 1 - self.x, self.core)
        self.copy(chunk, s, self.sibling, 0).wait_recv()

        @pl.when(jnp.logical_not(self.direct_to(step)))
        def _():
            self.copy(chunk, s, self.sibling, 13 + step).start()

    def relay(self, ends, middles=None):
        def run(names):
            for name in names:
                step, s = int(name[1]), int(name[2])
                if name[0] == "Z":
                    self.pass_z(step, s)
                else:
                    self.pass_x(step, s)

        if middles is None:
            run(ends)
            return
        middle = (self.z > 0) & (self.z < 3)

        @pl.when(middle)
        def _():
            run(middles)

        @pl.when(jnp.logical_not(middle))
        def _():
            run(ends)

    def take(self, step, sides=(0, 1)):
        for side in sides:
            x = 1 - self.x if side else self.x
            chunk = self.at(step, x, 1 - self.core)

            @pl.when(jnp.logical_not(self.crosses & (chunk == self.partner)))
            def _():
                for s in range(PARTS):
                    self.copy(chunk, s, self.sibling, 0).wait_recv()

    def drain(self):
        for s in range(PARTS):

            @pl.when(self.z < 3)
            def _():
                self.copy(self.me, s, self.sibling, 0).wait_send()

            @pl.when(self.z > 0)
            def _():
                self.copy(self.me, s, self.sibling, 1).wait_send()

            for step in range(1, 4):
                _, valid = self.along(step)

                @pl.when(valid)
                def _():
                    self.copy(self.me, s, self.sibling, 3 + step).wait_send()

            for step in range(1, 4):

                @pl.when(jnp.logical_not(self.direct_from(step)))
                def _():
                    self.copy(self.me, s, self.sibling, 6 + step).wait_send()

                @pl.when(jnp.logical_not(self.direct_to(step)))
                def _():
                    self.copy(self.me, s, self.sibling, 13 + step).wait_send()

            @pl.when(self.crosses)
            def _():
                self.copy(self.me, s, self.sibling, 17).wait_send()
                self.copy(self.me, s, self.sibling, 18).wait_send()

            if s == PARTS - 1 or not self.paced:
                self.copy(self.me, s, self.sibling, 2).wait_send()
            for index in (3, 10, 11, 12, 13):
                self.copy(self.me, s, self.sibling, index).wait_send()


def moved(values, offset, axis):
    extent = values.shape[axis]
    rolled = pltpu.roll(values, (-offset) % extent, axis)
    place = lax.broadcasted_iota(jnp.int32, values.shape, axis)
    return jnp.where(place == (extent - 1 if offset > 0 else 0), 0.0, rolled)


def iota(shape, axis):
    return lax.broadcasted_iota(jnp.int32, shape, axis)


def over_48(index):
    return ((index >> 4) * 171) >> 9


def along_face(values, offset):
    if offset == 0:
        return values
    rolled = pltpu.roll(values, (-offset) % values.shape[0], 0)
    place = (iota(values.shape, 0) & 7) + offset
    return jnp.where((place >= 0) & (place < 8), rolled, 0.0)


def dot(left, right):
    return jnp.dot(left, right, preferred_element_type=F32)


def dot_back(left, right):
    return lax.dot_general(left, right, (((1,), (1,)), ((), ())), preferred_element_type=F32)


def wide(values):
    return jnp.concatenate([values, values, values], axis=1)


def step_kernel(
    time_ref,
    owner_hbm,
    slot_hbm,
    count_hbm,
    faces_hbm,
    mask_hbm,
    gain_hbm,
    w1_hbm,
    w2_hbm,
    clean_hbm,
    noise_hbm,
    kernel_hbm,
    acc_ref,
    shifted,
    gbuf,
    small_ref,
    owner_ref,
    slot_ref,
    count_ref,
    faces_ref,
    mask_ref,
    gain_ref,
    w1_ref,
    w2_ref,
    clean_ref,
    noise_ref,
    kernel_ref,
    load_sems,
    sbuf,
    rbuf,
    x_send,
    x_recv,
    w1_dense,
    w2_dense,
    mixed,
    first_out,
    inputs,
    hiddens,
    chosen,
    inv_cov,
    inverse_ref,
    normed_ref,
    act_ref,
    abuf,
    a_send,
    a_recv,
    g_send,
    g_recv,
    small_out,
    small_in,
    s_send,
    s_recv,
    t_send,
    t_recv,
    half_send,
    half_recv,
):
    me = lax.axis_index("tile")
    barrier = pltpu.get_barrier_semaphore()
    for k in range(1, 16):
        pl.semaphore_signal(
            barrier, inc=1, device_id={"tile": lax.rem(me + k, 16)}, device_id_type=MESH
        )
    pairs = (
        (owner_hbm, owner_ref),
        (slot_hbm, slot_ref),
        (count_hbm, count_ref),
        (faces_hbm, faces_ref),
        (mask_hbm, mask_ref),
        (gain_hbm, gain_ref),
        (w1_hbm, w1_ref),
        (w2_hbm, w2_ref),
        (clean_hbm, clean_ref),
        (noise_hbm, noise_ref),
        (kernel_hbm, kernel_ref),
    )
    loads = [
        pltpu.make_async_copy(far, near, load_sems.at[i]) for i, (far, near) in enumerate(pairs)
    ]
    for load in loads:
        load.start()
    core = lax.rem(me, 2)
    pixels, channels = act_ref.shape
    faces = owner_ref.shape[1]

    for load in loads[:4]:
        load.wait()
    square = (faces, faces)
    diagonal = iota(square, 0) == iota(square, 1)
    owner_row = owner_ref[...].astype(F32)
    owner_col = jnp.sum(jnp.where(diagonal, owner_row, 0.0), axis=1, keepdims=True)
    earlier = (owner_col == owner_row) & (iota(square, 1) < iota(square, 0))
    within = jnp.sum(jnp.where(earlier, 1.0, 0.0), axis=1, keepdims=True)
    goes_to = owner_col * 16.0 + within * 8.0
    lines = 8 * faces
    of_face = iota((faces, lines), 0) == (iota((faces, lines), 1) >> 3)
    row_of = jnp.sum(jnp.where(of_face, goes_to, 0.0), axis=0, keepdims=True)
    row_of = row_of + (iota((1, lines), 1) & 7).astype(F32)
    packer = jnp.where(iota((256, lines), 0).astype(F32) == row_of, 1.0, 0.0).astype(BF16)
    mine = (iota((lines, faces), 0) >> 3) == iota((lines, faces), 1)
    slot_of = jnp.sum(
        jnp.where(mine, slot_ref[...].astype(F32), 0.0), axis=1, keepdims=True
    )
    count_of = jnp.sum(
        jnp.where(mine, count_ref[...].astype(F32), 0.0), axis=1, keepdims=True
    )
    pixel = (iota((lines, 1), 0) & 7).astype(F32)
    label = jnp.where(pixel < count_of, slot_of * 8.0 + pixel + 1.0, 0.0)
    sbuf[:, 0:16, :] = dot(packer, faces_ref[...]).astype(BF16).reshape(16, 16, 128)
    sbuf[:, 16:32, :] = (
        dot(packer, jnp.broadcast_to(label, (lines, 128)).astype(BF16))
        .astype(BF16)
        .reshape(16, 16, 128)
    )
    pl.semaphore_wait(barrier, 15)
    sends = []
    for k in range(1, 16):
        to = lax.rem(me + k, 16)
        send = pltpu.make_async_remote_copy(
            src_ref=sbuf.at[to],
            dst_ref=rbuf.at[me],
            send_sem=x_send.at[k - 1],
            recv_sem=x_recv.at[k - 1],
            device_id={"tile": to},
            device_id_type=MESH,
        )
        send.start()
        sends.append(send)
    rbuf[me] = sbuf[me]
    for load in loads[4:]:
        load.wait()
    spread = (
        iota((48, channels), 1) - 48 * over_48(iota((48, channels), 1)) == iota((48, channels), 0)
    )
    spread = jnp.where(spread, 1.0, 0.0).astype(BF16)
    group_of = over_48(iota((1, channels), 1))
    keep1 = (iota((128, 1), 0) >> 4) == group_of
    keep2 = over_48(iota((channels, 1), 0)) == group_of
    for k in range(3):
        dense = dot(w1_ref[k * 128 : (k + 1) * 128], spread)
        w1_dense[k] = jnp.where(keep1, dense, 0.0).astype(BF16)
        dense = dot(w2_ref[k * channels : (k + 1) * channels], spread)
        w2_dense[k] = jnp.where(keep2, dense, 0.0).astype(BF16)
    time_value = (jnp.full((1, channels), time_ref[0], jnp.int32).astype(F32) + 0.5) / NSTEPS
    mixed[...] = (1.0 - time_value) * noise_ref[...].astype(F32) + time_value * clean_ref[
        ...
    ].astype(F32)
    on_diagonal = iota((pixels, pixels), 0) == iota((pixels, pixels), 1)
    cloudy = jnp.where(on_diagonal, mask_ref[...].astype(F32), 0.0).astype(BF16)
    pixel_weight = (1.0 + dot(cloudy, jnp.ones((pixels, 128), BF16))) / pixels
    zero_pixels = jnp.zeros((3 * channels, pixels), BF16)
    shifted[:, 0:pixels] = zero_pixels
    shifted[:, 17 * pixels : 18 * pixels] = zero_pixels
    abuf[ZERO] = jnp.zeros((channels, pixels), BF16)
    gbuf[ZERO] = jnp.zeros((pixels, channels), BF16)
    for send in sends:
        send.wait()
    plain = rbuf[:, 0:16, :].reshape(256, 128).astype(F32)
    total = jnp.zeros((256, channels), F32)
    for k in range(3):
        inputs[k] = along_face(plain, k - 1).astype(BF16)
        total = total + dot(inputs[k], w1_dense[k])
    first_out[...] = total
    hidden = (total * jax.nn.sigmoid(total)).astype(BF16)
    hidden_wide = hidden.astype(F32)
    total = hidden_wide
    for k in range(3):
        hiddens[k] = along_face(hidden_wide, 2 * (k - 1)).astype(BF16)
        total = total + dot(hiddens[k], w2_dense[k])
    encoded = total.astype(BF16)
    labels = rbuf[:, 16:32, :].reshape(256, 128).astype(F32)
    hits = jnp.concatenate([labels, labels], axis=1) == (iota((256, pixels), 1) + 1).astype(F32)
    chosen[...] = jnp.where(hits, 1.0, 0.0).astype(BF16)
    placer = chosen[...].T
    inv_cov[...] = 1.0 / (1.0 + dot(placer, jnp.ones((256, 128), BF16)))
    hsum = mixed[...] + dot(placer, encoded) * wide(inv_cov[...])
    inverse = lax.rsqrt(jnp.mean(hsum * hsum, axis=1, keepdims=True) + epsilon)
    inverse_ref[...] = jnp.broadcast_to(inverse, (pixels, 128))
    normed_ref[...] = hsum * inverse
    lifted = normed_ref[...] * gain_ref[...].reshape(1, channels)
    act_ref[...] = (lifted * jax.nn.sigmoid(lifted)).astype(BF16)
    abuf[me] = act_ref[...].T
    acts = Gather(abuf, a_send, a_recv)
    acts.cross()
    acts.start(0)
    own = act_ref[...]
    sums = [dot(own, kernel_ref[3 + d]) for d in range(3)]
    acts.start(1)
    part = channels // 2
    half = pl.ds(pl.multiple_of(core * part, part), part)

    def shift_one(chunk):
        plain = abuf[chunk]
        values = plain.astype(F32)
        here = pl.ds(pl.multiple_of((chunk + 1) * pixels, pixels), pixels)
        shifted[0:channels, here] = moved(values, -1, 1).astype(BF16)
        shifted[channels : 2 * channels, here] = plain
        shifted[2 * channels : 3 * channels, here] = moved(values, 1, 1).astype(BF16)

    def shift_plane(order):
        base = acts.planes[order] * 4

        def step(i, carry):
            shift_one(base + i)
            return carry

        lax.fori_loop(0, 4, step, 0)

    def half_copy(row):
        return pltpu.make_async_remote_copy(
            src_ref=acc_ref.at[pl.ds(3 * row, 3), half],
            dst_ref=acc_ref.at[pl.ds(3 * row, 3), half],
            send_sem=half_send.at[row],
            recv_sem=half_recv.at[row],
            device_id={"tile": acts.sibling},
            device_id_type=MESH,
        )

    def multiply(order, row):
        base, count = acts.planes[order] * 4, 4
        right = gbuf[pl.ds(base, count)].reshape(count * pixels, channels)
        start = pl.multiple_of((base + row) * pixels, pixels)
        for d in range(3):
            rows = pl.ds(pl.multiple_of(d * channels + core * part, part), part)
            piece = dot(shifted[rows, pl.ds(start, count * pixels)], right)
            if order == 0:
                acc_ref[3 * row + d, half, :] = piece
            else:
                acc_ref[3 * row + d, half, :] = acc_ref[3 * row + d, half, :] + piece
        if order == 2:
            half_copy(row).start()

    acts.relay(("X00", "Z10", "X01", "Z11"), ("X00", "Z10", "Z20", "X01", "Z11", "Z21"))
    acts.take(0)
    acts.take_cross()
    above = abuf[jnp.where(me > 0, me - 1, ZERO)].T
    below = abuf[jnp.where(me < 15, me + 1, ZERO)].T
    sums = [
        sums[d] + dot(above, kernel_ref[d]) + dot(below, kernel_ref[6 + d]) for d in range(3)
    ]
    predicted = sums[1] + moved(sums[0], -1, 0) + moved(sums[2], 1, 0)
    grad = (
        wide(pixel_weight)
        * (predicted - clean_ref[...].astype(F32) + noise_ref[...].astype(F32))
    ).astype(BF16)
    gbuf[me] = grad
    grads = Gather(gbuf, g_send, g_recv, False)
    grads.cross()
    grads.start(0)
    grads.start(1)
    own = gbuf[me]
    sums = [dot_back(own, kernel_ref[3 + d]) for d in range(3)]
    acts.relay(("Z20", "X10"), ("Z30", "X10", "X20"))
    acts.relay(("Z21", "X11"), ("Z31", "X11", "X21"))
    shift_plane(0)
    grads.relay(("X00", "Z10", "X01", "Z11"), ("X00", "Z10", "Z20", "X01", "Z11", "Z21"))
    grads.take(0)
    grads.take_cross()
    above = gbuf[jnp.where(me > 0, me - 1, ZERO)]
    below = gbuf[jnp.where(me < 15, me + 1, ZERO)]
    sums = [
        sums[d] + dot_back(below, kernel_ref[d]) + dot_back(above, kernel_ref[6 + d])
        for d in range(3)
    ]
    flows = sums[1] + moved(sums[0], 1, 0) + moved(sums[2], -1, 0)
    acts.relay(("Z30", "X20", "Z31", "X21"), ())
    acts.take(1)
    shift_plane(1)

    gain = gain_ref[...].reshape(1, channels)
    normed = normed_ref[...]
    lifted = normed * gain
    logistic = jax.nn.sigmoid(lifted)
    grad_lift = flows * logistic * (1.0 + lifted * (1.0 - logistic))
    gain_part = jnp.sum(grad_lift * normed, axis=0, keepdims=True)
    grad_norm = grad_lift * gain
    grad_hsum = wide(inverse_ref[...]) * (
        grad_norm - normed * jnp.mean(grad_norm * normed, axis=1, keepdims=True)
    )
    scaled = (grad_hsum * wide(inv_cov[...])).astype(BF16)
    cotangent_wide = dot(chosen[...], scaled)
    cotangent = cotangent_wide.astype(BF16)
    grad_hidden = cotangent_wide
    small_rows = []
    for k in range(3):
        grad_hidden = grad_hidden + dot_back(
            along_face(cotangent_wide, -2 * (k - 1)).astype(BF16), w2_dense[k]
        )
        product = jnp.where(keep2, dot(hiddens[k].T, cotangent), 0.0)
        small_rows.append(sum(product[48 * g : 48 * (g + 1)] for g in range(8)))
    logistic = jax.nn.sigmoid(first_out[...])
    grad_first = grad_hidden * logistic * (1.0 + first_out[...] * (1.0 - logistic))
    grad_high = grad_first.astype(BF16)
    grad_low = (grad_first - grad_high.astype(F32)).astype(BF16)
    for k in range(3):
        turned = inputs[k].T
        product = jnp.where(keep1, dot(turned, grad_high) + dot(turned, grad_low), 0.0)
        small_rows.append(sum(product[16 * g : 16 * (g + 1)] for g in range(8)))
    small_rows.append(
        jnp.where(iota((16, channels), 0) == 0, jnp.broadcast_to(gain_part, (16, channels)), 0.0)
    )
    small_out[...] = jnp.concatenate(small_rows, axis=0).astype(BF16)
    def small_send(k):
        to = lax.rem(me + k, 16)
        rows = pl.ds(pl.multiple_of(jnp.minimum(to, 12) * 16, 16), 16)
        return to < 13, pltpu.make_async_remote_copy(
            src_ref=small_out.at[rows],
            dst_ref=small_in.at[me],
            send_sem=s_send.at[k - 1],
            recv_sem=s_recv.at[k - 1],
            device_id={"tile": to},
            device_id_type=MESH,
        )

    my_rows = pl.ds(pl.multiple_of(jnp.minimum(me, 12) * 16, 16), 16)

    def small_spread(k):
        return pltpu.make_async_remote_copy(
            src_ref=small_ref.at[my_rows],
            dst_ref=small_ref.at[my_rows],
            send_sem=t_send.at[k - 1],
            recv_sem=t_recv.at[k - 1],
            device_id={"tile": lax.rem(me + k, 16)},
            device_id_type=MESH,
        )

    for k in range(1, 16):
        valid, send = small_send(k)

        @pl.when(valid)
        def _():
            send.start()

    grads.relay(("Z20", "X10"), ("Z30", "X10", "X20"))
    acts.relay(("X30", "X31"))
    acts.take(2)
    shift_plane(2)
    grads.relay(("Z21", "X11"), ("Z31", "X11", "X21"))
    multiply(0, 0)
    multiply(0, 1)
    acts.take(3)
    grads.relay(("Z30", "X20"), ())
    multiply(0, 2)
    shift_plane(3)
    grads.relay(("Z31", "X21"), ())
    grads.take(1)
    multiply(1, 0)

    multiply(1, 1)
    multiply(1, 2)
    grads.take(2)
    @pl.when(me < 13)
    def _():
        for k in range(1, 16):
            small_send(k)[1].wait_recv()
        small_in[me] = small_out[my_rows, :]
        added = small_in[0].astype(F32)
        for k in range(1, 16):
            added = added + small_in[k].astype(F32)
        small_ref[my_rows, :] = added.astype(BF16)
        for k in range(1, 16):
            small_spread(k).start()

    grads.relay(("X30",))
    multiply(2, 0)
    multiply(2, 1)
    multiply(2, 2)
    grads.relay(("X31",))
    for k in range(1, 16):

        @pl.when(lax.rem(me + 16 - k, 16) < 13)
        def _():
            small_spread(k).wait_recv()

    grads.take(3)
    for row in range(3):
        half_copy(row).wait()

    @pl.when(me < 13)
    def _():
        for k in range(1, 16):
            small_spread(k).wait_send()

    for k in range(1, 16):
        valid, send = small_send(k)

        @pl.when(valid)
        def _():
            send.wait_send()

    acts.drain()
    grads.drain()


def step_call(
    time_index, owner, slot, count, faces, mask, gain, first_w, second_w, clean, noise, kernel
):
    pixels, channels = clean.shape
    dma = pltpu.SemaphoreType.DMA
    whole = pl.BlockSpec(memory_space=VM)
    staged = (owner, slot, count, faces, mask, gain, first_w, second_w, clean, noise, kernel)
    staged = tuple(pltpu.with_memory_space_constraint(array, pltpu.HBM) for array in staged)
    return pl.pallas_call(
        step_kernel,
        out_shape=(
            jax.ShapeDtypeStruct((9, channels, channels), F32),
            jax.ShapeDtypeStruct((3 * channels, 18 * pixels), BF16),
            jax.ShapeDtypeStruct((17, pixels, channels), BF16),
            jax.ShapeDtypeStruct((208, channels), BF16),
        ),
        in_specs=[pl.BlockSpec(memory_space=pltpu.SMEM)]
        + [pl.BlockSpec(memory_space=ANY)] * len(staged),
        out_specs=(whole,) * 4,
        scratch_shapes=[VM(array.shape, array.dtype) for array in staged]
        + [
            dma((len(staged),)),
            VM((16, 32, 128), BF16),
            VM((16, 32, 128), BF16),
            dma((15,)),
            dma((15,)),
            VM((3, 128, channels), BF16),
            VM((3, channels, channels), BF16),
            VM((pixels, channels), F32),
            VM((256, channels), F32),
            VM((3, 256, 128), BF16),
            VM((3, 256, channels), BF16),
            VM((256, pixels), BF16),
            VM((pixels, 128), F32),
            VM((pixels, 128), F32),
            VM((pixels, channels), F32),
            VM((pixels, channels), BF16),
            VM((17, channels, pixels), BF16),
            dma((19 * PARTS,)),
            dma((16, PARTS)),
            dma((19 * PARTS,)),
            dma((16, PARTS)),
            VM((208, channels), BF16),
            VM((16, 16, channels), BF16),
            dma((15,)),
            dma((15,)),
            dma((15,)),
            dma((15,)),
            dma((3,)),
            dma((3,)),
        ],
        compiler_params=pltpu.CompilerParams(
            collective_id=0, has_side_effects=True, vmem_limit_bytes=28 * 2**20
        ),
        name="step",
    )(time_index, *staged)


def finish_kernel(
    acc_ref, shifted, gbuf, small_ref, kernel_out, gain_out, first_out, second_out, held, sems
):
    me = lax.axis_index("tile")
    channels = acc_ref.shape[1]
    pixels = gbuf.shape[1]
    z = me // 4
    base = 4 * jnp.where(z < 2, 3, 0)
    right = gbuf[pl.ds(base, 4)].reshape(4 * pixels, channels)

    def step(row, carry):
        start = pl.multiple_of((base + row) * pixels, pixels)
        for d in range(3):
            tap = 3 * row + d
            left = shifted[d * channels : (d + 1) * channels, pl.ds(start, 4 * pixels)]
            held[tap] = acc_ref[tap] + dot(left, right)
            pltpu.make_async_copy(held.at[tap], kernel_out.at[tap], sems.at[tap]).start()
        return carry

    lax.fori_loop(0, 3, step, 0)
    summed = small_ref[...].astype(F32)
    for k in range(3):
        second = summed[48 * k : 48 * (k + 1)]
        first = summed[144 + 16 * k : 144 + 16 * (k + 1)]
        for g in range(8):
            turn = (channels - 48 * g) % channels
            turned = pltpu.roll(second, turn, 1)[:, :48] if turn else second[:, :48]
            second_out[(8 * k + g) * 48 : (8 * k + g + 1) * 48, :] = turned
            turned = pltpu.roll(first, turn, 1)[:, :48] if turn else first[:, :48]
            first_out[(8 * k + g) * 16 : (8 * k + g + 1) * 16, :] = turned
    gain_out[...] = summed[192]
    for tap in range(9):
        pltpu.make_async_copy(held.at[tap], kernel_out.at[tap], sems.at[tap]).wait()


def finish_call(acc, shifted, grads, small):
    channels = acc.shape[1]
    whole = pl.BlockSpec(memory_space=VM)
    return pl.pallas_call(
        finish_kernel,
        out_shape=(
            jax.ShapeDtypeStruct(acc.shape, F32),
            jax.ShapeDtypeStruct((channels,), F32),
            jax.ShapeDtypeStruct((384, 48), F32),
            jax.ShapeDtypeStruct((1152, 48), F32),
        ),
        in_specs=[whole] * 4,
        out_specs=(pl.BlockSpec(memory_space=ANY), whole, whole, whole),
        scratch_shapes=[VM(acc.shape, F32), pltpu.SemaphoreType.DMA((9,))],
        compiler_params=pltpu.CompilerParams(vmem_limit_bytes=12 * 2**20),
        name="finish",
    )(acc, shifted, grads, small)


def body16(
    sar_faces,
    dest_owner,
    face_slot,
    valid_pixels,
    cloud_mask,
    time_index,
    clean_latent,
    noise_latent,
    encoder_first,
    encoder_second,
    conv_kernel,
    norm_gain,
):
    channels_in = sar_faces.shape[-1]
    channels = clean_latent.shape[-1]
    acc, shifted, grads, small = step_call(
        time_index,
        dest_owner.reshape(1, -1),
        face_slot.reshape(1, -1),
        valid_pixels.reshape(1, -1),
        sar_faces.reshape(-1, channels_in),
        cloud_mask,
        norm_gain,
        encoder_first.reshape(-1, encoder_first.shape[-1]),
        encoder_second.reshape(-1, encoder_second.shape[-1]),
        clean_latent.reshape(-1, channels),
        noise_latent.reshape(-1, channels),
        conv_kernel,
    )
    grad_kernel, grad_gain, grad_first, grad_second = finish_call(acc, shifted, grads, small)
    return (
        grad_kernel,
        grad_gain,
        grad_first.reshape(encoder_first.shape),
        grad_second.reshape(encoder_second.shape),
    )


def body(
    sar_faces,
    dest_owner,
    face_slot,
    valid_pixels,
    cloud_mask,
    time_index,
    clean_latent,
    noise_latent,
    encoder_first,
    encoder_second,
    conv_kernel,
    norm_gain,
):
    owners = lax.axis_size("tile")
    slot_total = owners * MOST
    face_count, length, channels_in = sar_faces.shape
    rows, columns, channels = clean_latent.shape
    tile_faces = rows * columns // length
    owner_list = dest_owner[:, 0]
    order = jnp.arange(face_count, dtype=jnp.int32)
    within = jnp.sum(
        (
            (owner_list[:, None] == owner_list[None, :]) & (order[None, :] < order[:, None])
        ).astype(jnp.int32),
        axis=1,
    )
    buffer_at = owner_list * MOST + within
    placed = (jnp.arange(slot_total, dtype=jnp.int32)[:, None] == buffer_at[None, :]).astype(
        jnp.int32
    )
    placer = placed.astype(jnp.bfloat16)
    labels = jnp.stack(
        [
            jnp.sum(placed * face_slot[None, :], axis=1),
            jnp.sum(placed * valid_pixels[None, :], axis=1),
        ],
        axis=-1,
    )
    labels = labels.reshape(owners, MOST, 2)
    packed = jnp.einsum(
        "sf,fjc->sjc", placer, sar_faces, preferred_element_type=jnp.float32
    ).astype(jnp.bfloat16)
    arrived, recv_labels = (
        lax.all_to_all(
            packed.reshape(owners, MOST, length, channels_in),
            "tile",
            split_axis=0,
            concat_axis=0,
            tiled=True,
        ),
        lax.all_to_all(labels, "tile", split_axis=0, concat_axis=0, tiled=True),
    )
    raw_slots = arrived.reshape(slot_total, length, channels_in)
    received, saved = encoder_forward(raw_slots, encoder_first, encoder_second)
    recv_labels = recv_labels.reshape(slot_total, 2)
    recv_slot = recv_labels[:, 0]
    recv_count = recv_labels[:, 1]
    validity = (jnp.arange(length, dtype=jnp.int32)[None, :] < recv_count[:, None]).astype(
        jnp.float32
    )
    selector = recv_slot[:, None] == jnp.arange(tile_faces, dtype=jnp.int32)[None, :]
    masked = received * validity[..., None].astype(jnp.bfloat16)
    summed = jnp.einsum(
        "sp,sjc->pjc", selector.astype(jnp.bfloat16), masked, preferred_element_type=jnp.float32
    )
    covered = jnp.einsum(
        "sp,sj->pj", selector.astype(jnp.float32), validity, precision=highest
    ).reshape(-1, 1)
    condition = summed.reshape(-1, channels) / (1.0 + covered)
    time_value = (time_index[0].astype(jnp.float32) + 0.5) / NSTEPS
    noise_flat = noise_latent.astype(jnp.float32).reshape(-1, channels)
    clean_flat = clean_latent.astype(jnp.float32).reshape(-1, channels)
    hsum = (1.0 - time_value) * noise_flat + time_value * clean_flat + condition
    inverse = lax.rsqrt(jnp.mean(hsum * hsum, axis=-1, keepdims=True) + epsilon)
    normed = hsum * inverse
    lifted = normed * norm_gain
    activated = jax.nn.silu(lifted).astype(jnp.bfloat16).reshape(rows, columns, channels)
    extended = with_halo(activated, (("tile", 0),), 1)
    padded = jnp.pad(extended, ((0, 0), (1, 1), (0, 0)))
    predicted = convolve_forward(padded, conv_kernel, rows, columns)
    pixel_weight = (1 + cloud_mask).astype(jnp.float32).reshape(-1, 1)
    grad_pred = (pixel_weight * (predicted - clean_flat + noise_flat) / (rows * columns)).astype(
        jnp.bfloat16
    )
    grad_rows = with_halo(grad_pred.reshape(rows, columns, channels), (("tile", 0),), 1)
    padded_grad = jnp.pad(grad_rows, ((0, 0), (1, 1), (0, 0)))
    flows, kernel_part = convolve_backward(padded, padded_grad, conv_kernel, rows, columns)
    gain_part, grad_hsum = norm_backward(flows, lifted, normed, inverse, norm_gain)
    scaled = (grad_hsum / (1.0 + covered)).astype(jnp.bfloat16)
    target = recv_slot[:, None] * length + jnp.arange(length, dtype=jnp.int32)[None, :]
    target = jnp.where(validity > 0, target, -1).reshape(-1)
    picker = target[:, None] == jnp.arange(rows * columns, dtype=jnp.int32)[None, :]
    slot_grads = jnp.dot(
        picker.astype(jnp.bfloat16), scaled, preferred_element_type=jnp.float32
    ).astype(jnp.bfloat16)
    slot_grads = slot_grads.reshape(slot_total, length, channels)
    first_part, second_part = encoder_backward(saved, slot_grads, encoder_first, encoder_second)
    reduced = lax.psum((kernel_part, gain_part, first_part, second_part), "tile")
    return (reduced[0], reduced[1], reduced[2], reduced[3])


def solution(mesh):
    placed = (
        P(("groups", "tile"), None, None),
        P(("groups", "tile"), None),
        P(("groups", "tile")),
        P(("groups", "tile")),
        P(("groups", "tile"), None),
        P(("groups", "tile")),
        P(("groups", "tile"), None, None),
        P(("groups", "tile"), None, None),
        P(),
        P(),
        P(),
        P(),
    )
    return jax.shard_map(
        body16 if mesh.shape["tile"] == 16 else body,
        mesh=mesh,
        in_specs=placed,
        out_specs=(
            P("groups", None, None),
            P("groups"),
            P("groups", None, None, None),
            P("groups", None, None, None),
        ),
        check_vma=False,
    )
```

```python
import jax
import jax.numpy as jnp
from jax import lax
from jax.experimental import pallas as pl
from jax.experimental.pallas import tpu as pltpu
from jax.sharding import PartitionSpec as P

MOST = 2
NSTEPS = 1000


highest = lax.Precision.HIGHEST
epsilon = 1e-06


def with_halo(block, sides, width):
    for axis, dim in sides:
        count = lax.axis_size(axis)
        forward = [(i, i + 1) for i in range(count - 1)]
        backward = [(target, source) for source, target in forward]
        low = lax.ppermute(
            lax.slice_in_dim(block, block.shape[dim] - width, None, axis=dim), axis, forward
        )
        high = lax.ppermute(lax.slice_in_dim(block, 0, width, axis=dim), axis, backward)
        block = jnp.concatenate([low, block, high], axis=dim)
    return block


def shift_line(values, offset):
    if offset == 0:
        return values
    zeros = jnp.zeros_like(values[:, : abs(offset)])
    if offset > 0:
        return jnp.concatenate([values[:, offset:], zeros], axis=1)
    return jnp.concatenate([zeros, values[:, :offset]], axis=1)


def taps_forward(inputs, weight, spread):
    summed = jnp.zeros(inputs.shape[:3] + (weight.shape[-1],), jnp.float32)
    for shift_tap in range(3):
        shifted = shift_line(inputs, (shift_tap - 1) * spread)
        summed = summed + jnp.einsum(
            "flgi,gio->flgo", shifted, weight[shift_tap], preferred_element_type=jnp.float32
        )
    return summed


def taps_weight_grad(inputs, cotangent, spread, exact):
    pieces = []
    for shift_tap in range(3):
        shifted = shift_line(inputs, (shift_tap - 1) * spread)
        if exact:
            pieces.append(
                jnp.einsum(
                    "flgi,flgo->gio", shifted.astype(jnp.float32), cotangent, precision=highest
                )
            )
        else:
            pieces.append(
                jnp.einsum("flgi,flgo->gio", shifted, cotangent, preferred_element_type=jnp.float32)
            )
    return jnp.stack(pieces)


def taps_input_grad(cotangent, weight, spread):
    summed = jnp.zeros(cotangent.shape[:3] + (weight.shape[2],), jnp.float32)
    for shift_tap in range(3):
        moved = jnp.einsum(
            "flgo,gio->flgi", cotangent, weight[shift_tap], preferred_element_type=jnp.float32
        )
        summed = summed + shift_line(moved, -(shift_tap - 1) * spread)
    return summed


def encoder_forward(sar_faces, first_w, second_w):
    face_count, length, channels_in = sar_faces.shape
    groups = first_w.shape[1]
    inputs = sar_faces.reshape(face_count, length, groups, -1)
    first_out = taps_forward(inputs, first_w, 1)
    hidden = jax.nn.silu(first_out).astype(jnp.bfloat16)
    second = taps_forward(hidden, second_w, 2)
    encoded = (
        (hidden.astype(jnp.float32) + second).reshape(face_count, length, -1).astype(jnp.bfloat16)
    )
    return (encoded, (inputs, first_out, hidden))


def encoder_backward(saved, grad_face, first_w, second_w):
    inputs, first_out, hidden = saved
    groups = first_w.shape[1]
    face_count, length, channels = grad_face.shape
    cotangent = grad_face.reshape(face_count, length, groups, -1)
    second_part = taps_weight_grad(hidden, cotangent, 2, False)
    grad_hidden = cotangent.astype(jnp.float32) + taps_input_grad(cotangent, second_w, 2)
    logistic = jax.nn.sigmoid(first_out)
    grad_first_out = grad_hidden * logistic * (1.0 + first_out * (1.0 - logistic))
    first_part = taps_weight_grad(inputs, grad_first_out, 1, True)
    return (first_part, second_part)


def convolve_forward(padded, kernel, rows, columns):
    channels = kernel.shape[-1]
    summed = jnp.zeros((rows * columns, channels), jnp.float32)
    for row_tap in range(3):
        for col_tap in range(3):
            window = padded[row_tap : row_tap + rows, col_tap : col_tap + columns].reshape(
                -1, channels
            )
            summed = summed + jnp.dot(
                window, kernel[3 * row_tap + col_tap], preferred_element_type=jnp.float32
            )
    return summed


def convolve_backward(padded_act, padded_grad, kernel, rows, columns):
    channels = kernel.shape[-1]
    incoming = padded_grad[1 : rows + 1, 1 : columns + 1].reshape(-1, channels)
    flows = jnp.zeros((rows * columns, channels), jnp.float32)
    kernels = []
    for row_tap in range(3):
        for col_tap in range(3):
            window = padded_act[row_tap : row_tap + rows, col_tap : col_tap + columns].reshape(
                -1, channels
            )
            kernels.append(
                lax.dot_general(
                    window, incoming, (((0,), (0,)), ((), ())), preferred_element_type=jnp.float32
                )
            )
            moved = padded_grad[
                2 - row_tap : 2 - row_tap + rows, 2 - col_tap : 2 - col_tap + columns
            ].reshape(-1, channels)
            flows = flows + lax.dot_general(
                moved,
                kernel[3 * row_tap + col_tap],
                (((1,), (1,)), ((), ())),
                preferred_element_type=jnp.float32,
            )
    return (flows, jnp.stack(kernels))


def norm_backward(flows, lifted, normed, inverse, gain):
    logistic = jax.nn.sigmoid(lifted)
    grad_lift = flows * logistic * (1.0 + lifted * (1.0 - logistic))
    gain_part = jnp.sum(grad_lift * normed, axis=0)
    grad_norm = grad_lift * gain
    grad_hsum = inverse * (
        grad_norm - normed * jnp.mean(grad_norm * normed, axis=-1, keepdims=True)
    )
    return (gain_part, grad_hsum)


MESH = pl.DeviceIdType.MESH
VM = pltpu.VMEM
ANY = pl.ANY
F32 = jnp.float32
BF16 = jnp.bfloat16
ZERO = 16
PARTS = 2


class Gather:
    def __init__(self, buf, send, recv, paced=True):
        self.paced = paced
        self.buf, self.send_sem, self.recv_sem = buf, send, recv
        self.rows = buf.shape[1] // PARTS
        self.me = lax.axis_index("tile")
        self.core = lax.rem(self.me, 2)
        self.x = lax.rem(self.me // 2, 2)
        self.z = z = self.me // 4
        self.x_peer = z * 4 + (1 - self.x) * 2 + self.core
        self.sibling = z * 4 + self.x * 2 + (1 - self.core)
        self.planes = [
            z,
            jnp.where(z == 0, 1, z - 1),
            jnp.where(z == 0, 2, jnp.where(z == 3, 1, z + 1)),
            jnp.where(z < 2, 3, 0),
        ]
        place = lax.rem(self.me, 4)
        self.crosses = ((place == 0) & (z > 0)) | ((place == 3) & (z < 3))
        self.partner = jnp.where(place == 0, jnp.maximum(self.me - 1, 0), jnp.minimum(self.me + 1, 15))

    def direct_from(self, step):
        plane = self.planes[step]
        return ((plane == self.z + 1) & (self.x == 0) & (self.core == 0)) | (
            (plane == self.z - 1) & (self.x == 1) & (self.core == 1)
        )

    def direct_to(self, step):
        plane = self.planes[step]
        return ((plane == self.z + 1) & (self.x == 1) & (self.core == 0)) | (
            (plane == self.z - 1) & (self.x == 0) & (self.core == 1)
        )

    def cross(self):
        @pl.when(self.crosses)
        def _():
            for s in range(PARTS):
                self.copy(self.me, s, self.partner, 17).start()

    def take_cross(self):
        @pl.when(self.crosses)
        def _():
            for s in range(PARTS):
                self.copy(self.partner, s, self.sibling, 18).wait_recv()
                self.copy(self.partner, s, self.sibling, 18).start()

    def copy(self, chunk, s, to, index):
        part = self.buf.at[chunk, pl.ds(s * self.rows, self.rows)]
        return pltpu.make_async_remote_copy(
            src_ref=part,
            dst_ref=part,
            send_sem=self.send_sem.at[index * PARTS + s],
            recv_sem=self.recv_sem.at[chunk, s],
            device_id={"tile": to},
            device_id_type=MESH,
        )

    def at(self, step, x, core):
        return self.planes[step] * 4 + x * 2 + core

    def along(self, step):
        onward = jnp.where(self.planes[step] < self.z, self.z + 1, self.z - 1)
        valid = (onward >= 0) & (onward <= 3)
        return jnp.clip(onward, 0, 3) * 4 + lax.rem(self.me, 4), valid

    def start(self, s):
        place = lax.rem(self.me, 4)
        if s and self.paced:
            self.copy(self.me, s - 1, self.x_peer, 2).wait_send()

        @pl.when(self.z < 3)
        def _():
            self.copy(self.me, s, jnp.minimum(self.z + 1, 3) * 4 + place, 0).start()

        @pl.when(self.z > 0)
        def _():
            self.copy(self.me, s, jnp.maximum(self.z - 1, 0) * 4 + place, 1).start()

        self.copy(self.me, s, self.x_peer, 2).start()
        self.copy(self.me, s, self.sibling, 3).start()

    def pass_z(self, step, s):
        chunk = self.at(step, self.x, self.core)
        self.copy(chunk, s, self.x_peer, 0).wait_recv()
        to, valid = self.along(step)

        @pl.when(valid)
        def _():
            self.copy(chunk, s, to, 3 + step).start()

        @pl.when(jnp.logical_not(self.direct_from(step)))
        def _():
            self.copy(chunk, s, self.x_peer, 6 + step).start()

        self.copy(chunk, s, self.sibling, 9 + step).start()

    def pass_x(self, step, s):
        chunk = self.at(step, 1 - self.x, self.core)
        self.copy(chunk, s, self.sibling, 0).wait_recv()

        @pl.when(jnp.logical_not(self.direct_to(step)))
        def _():
            self.copy(chunk, s, self.sibling, 13 + step).start()

    def relay(self, ends, middles=None):
        def run(names):
            for name in names:
                step, s = int(name[1]), int(name[2])
                if name[0] == "Z":
                    self.pass_z(step, s)
                else:
                    self.pass_x(step, s)

        if middles is None:
            run(ends)
            return
        middle = (self.z > 0) & (self.z < 3)

        @pl.when(middle)
        def _():
            run(middles)

        @pl.when(jnp.logical_not(middle))
        def _():
            run(ends)

    def take(self, step, sides=(0, 1)):
        for side in sides:
            x = 1 - self.x if side else self.x
            chunk = self.at(step, x, 1 - self.core)

            @pl.when(jnp.logical_not(self.crosses & (chunk == self.partner)))
            def _():
                for s in range(PARTS):
                    self.copy(chunk, s, self.sibling, 0).wait_recv()

    def drain(self):
        for s in range(PARTS):

            @pl.when(self.z < 3)
            def _():
                self.copy(self.me, s, self.sibling, 0).wait_send()

            @pl.when(self.z > 0)
            def _():
                self.copy(self.me, s, self.sibling, 1).wait_send()

            for step in range(1, 4):
                _, valid = self.along(step)

                @pl.when(valid)
                def _():
                    self.copy(self.me, s, self.sibling, 3 + step).wait_send()

            for step in range(1, 4):

                @pl.when(jnp.logical_not(self.direct_from(step)))
                def _():
                    self.copy(self.me, s, self.sibling, 6 + step).wait_send()

                @pl.when(jnp.logical_not(self.direct_to(step)))
                def _():
                    self.copy(self.me, s, self.sibling, 13 + step).wait_send()

            @pl.when(self.crosses)
            def _():
                self.copy(self.me, s, self.sibling, 17).wait_send()
                self.copy(self.me, s, self.sibling, 18).wait_send()

            if s == PARTS - 1 or not self.paced:
                self.copy(self.me, s, self.sibling, 2).wait_send()
            for index in (3, 10, 11, 12, 13):
                self.copy(self.me, s, self.sibling, index).wait_send()


def moved(values, offset, axis):
    extent = values.shape[axis]
    rolled = pltpu.roll(values, (-offset) % extent, axis)
    place = lax.broadcasted_iota(jnp.int32, values.shape, axis)
    return jnp.where(place == (extent - 1 if offset > 0 else 0), 0.0, rolled)


def iota(shape, axis):
    return lax.broadcasted_iota(jnp.int32, shape, axis)


def over_48(index):
    return ((index >> 4) * 171) >> 9


def along_face(values, offset):
    if offset == 0:
        return values
    rolled = pltpu.roll(values, (-offset) % values.shape[0], 0)
    place = (iota(values.shape, 0) & 7) + offset
    return jnp.where((place >= 0) & (place < 8), rolled, 0.0)


def dot(left, right):
    return jnp.dot(left, right, preferred_element_type=F32)


def dot_back(left, right):
    return lax.dot_general(left, right, (((1,), (1,)), ((), ())), preferred_element_type=F32)


def wide(values):
    return jnp.concatenate([values, values, values], axis=1)


def step_kernel(
    time_ref,
    owner_hbm,
    slot_hbm,
    count_hbm,
    faces_hbm,
    mask_hbm,
    gain_hbm,
    w1_hbm,
    w2_hbm,
    clean_hbm,
    noise_hbm,
    kernel_hbm,
    acc_ref,
    shifted,
    gbuf,
    small_ref,
    owner_ref,
    slot_ref,
    count_ref,
    faces_ref,
    mask_ref,
    gain_ref,
    w1_ref,
    w2_ref,
    clean_ref,
    noise_ref,
    kernel_ref,
    load_sems,
    sbuf,
    rbuf,
    x_send,
    x_recv,
    w1_dense,
    w2_dense,
    mixed,
    first_out,
    inputs,
    hiddens,
    chosen,
    inv_cov,
    inverse_ref,
    normed_ref,
    act_ref,
    abuf,
    a_send,
    a_recv,
    g_send,
    g_recv,
    small_out,
    small_in,
    s_send,
    s_recv,
    t_send,
    t_recv,
    half_send,
    half_recv,
):
    me = lax.axis_index("tile")
    barrier = pltpu.get_barrier_semaphore()
    for k in range(1, 16):
        pl.semaphore_signal(
            barrier, inc=1, device_id={"tile": lax.rem(me + k, 16)}, device_id_type=MESH
        )
    pairs = (
        (owner_hbm, owner_ref),
        (slot_hbm, slot_ref),
        (count_hbm, count_ref),
        (faces_hbm, faces_ref),
        (mask_hbm, mask_ref),
        (gain_hbm, gain_ref),
        (w1_hbm, w1_ref),
        (w2_hbm, w2_ref),
        (clean_hbm, clean_ref),
        (noise_hbm, noise_ref),
        (kernel_hbm, kernel_ref),
    )
    loads = [
        pltpu.make_async_copy(far, near, load_sems.at[i]) for i, (far, near) in enumerate(pairs)
    ]
    for load in loads:
        load.start()
    core = lax.rem(me, 2)
    pixels, channels = act_ref.shape
    faces = owner_ref.shape[1]

    for load in loads[:4]:
        load.wait()
    square = (faces, faces)
    diagonal = iota(square, 0) == iota(square, 1)
    owner_row = owner_ref[...].astype(F32)
    owner_col = jnp.sum(jnp.where(diagonal, owner_row, 0.0), axis=1, keepdims=True)
    earlier = (owner_col == owner_row) & (iota(square, 1) < iota(square, 0))
    within = jnp.sum(jnp.where(earlier, 1.0, 0.0), axis=1, keepdims=True)
    goes_to = owner_col * 16.0 + within * 8.0
    lines = 8 * faces
    of_face = iota((faces, lines), 0) == (iota((faces, lines), 1) >> 3)
    row_of = jnp.sum(jnp.where(of_face, goes_to, 0.0), axis=0, keepdims=True)
    row_of = row_of + (iota((1, lines), 1) & 7).astype(F32)
    packer = jnp.where(iota((256, lines), 0).astype(F32) == row_of, 1.0, 0.0).astype(BF16)
    mine = (iota((lines, faces), 0) >> 3) == iota((lines, faces), 1)
    slot_of = jnp.sum(
        jnp.where(mine, slot_ref[...].astype(F32), 0.0), axis=1, keepdims=True
    )
    count_of = jnp.sum(
        jnp.where(mine, count_ref[...].astype(F32), 0.0), axis=1, keepdims=True
    )
    pixel = (iota((lines, 1), 0) & 7).astype(F32)
    label = jnp.where(pixel < count_of, slot_of * 8.0 + pixel + 1.0, 0.0)
    sbuf[:, 0:16, :] = dot(packer, faces_ref[...]).astype(BF16).reshape(16, 16, 128)
    sbuf[:, 16:32, :] = (
        dot(packer, jnp.broadcast_to(label, (lines, 128)).astype(BF16))
        .astype(BF16)
        .reshape(16, 16, 128)
    )
    pl.semaphore_wait(barrier, 15)
    sends = []
    for k in range(1, 16):
        to = lax.rem(me + k, 16)
        send = pltpu.make_async_remote_copy(
            src_ref=sbuf.at[to],
            dst_ref=rbuf.at[me],
            send_sem=x_send.at[k - 1],
            recv_sem=x_recv.at[k - 1],
            device_id={"tile": to},
            device_id_type=MESH,
        )
        send.start()
        sends.append(send)
    rbuf[me] = sbuf[me]
    for load in loads[4:]:
        load.wait()
    spread = (
        iota((48, channels), 1) - 48 * over_48(iota((48, channels), 1)) == iota((48, channels), 0)
    )
    spread = jnp.where(spread, 1.0, 0.0).astype(BF16)
    group_of = over_48(iota((1, channels), 1))
    keep1 = (iota((128, 1), 0) >> 4) == group_of
    keep2 = over_48(iota((channels, 1), 0)) == group_of
    for k in range(3):
        dense = dot(w1_ref[k * 128 : (k + 1) * 128], spread)
        w1_dense[k] = jnp.where(keep1, dense, 0.0).astype(BF16)
        dense = dot(w2_ref[k * channels : (k + 1) * channels], spread)
        w2_dense[k] = jnp.where(keep2, dense, 0.0).astype(BF16)
    time_value = (jnp.full((1, channels), time_ref[0], jnp.int32).astype(F32) + 0.5) / NSTEPS
    mixed[...] = (1.0 - time_value) * noise_ref[...].astype(F32) + time_value * clean_ref[
        ...
    ].astype(F32)
    on_diagonal = iota((pixels, pixels), 0) == iota((pixels, pixels), 1)
    cloudy = jnp.where(on_diagonal, mask_ref[...].astype(F32), 0.0).astype(BF16)
    pixel_weight = (1.0 + dot(cloudy, jnp.ones((pixels, 128), BF16))) / pixels
    zero_pixels = jnp.zeros((3 * channels, pixels), BF16)
    shifted[:, 0:pixels] = zero_pixels
    shifted[:, 17 * pixels : 18 * pixels] = zero_pixels
    abuf[ZERO] = jnp.zeros((channels, pixels), BF16)
    gbuf[ZERO] = jnp.zeros((pixels, channels), BF16)
    for send in sends:
        send.wait()
    plain = rbuf[:, 0:16, :].reshape(256, 128).astype(F32)
    total = jnp.zeros((256, channels), F32)
    for k in range(3):
        inputs[k] = along_face(plain, k - 1).astype(BF16)
        total = total + dot(inputs[k], w1_dense[k])
    first_out[...] = total
    hidden = (total * jax.nn.sigmoid(total)).astype(BF16)
    hidden_wide = hidden.astype(F32)
    total = hidden_wide
    for k in range(3):
        hiddens[k] = along_face(hidden_wide, 2 * (k - 1)).astype(BF16)
        total = total + dot(hiddens[k], w2_dense[k])
    encoded = total.astype(BF16)
    labels = rbuf[:, 16:32, :].reshape(256, 128).astype(F32)
    hits = jnp.concatenate([labels, labels], axis=1) == (iota((256, pixels), 1) + 1).astype(F32)
    chosen[...] = jnp.where(hits, 1.0, 0.0).astype(BF16)
    placer = chosen[...].T
    inv_cov[...] = 1.0 / (1.0 + dot(placer, jnp.ones((256, 128), BF16)))
    hsum = mixed[...] + dot(placer, encoded) * wide(inv_cov[...])
    inverse = lax.rsqrt(jnp.mean(hsum * hsum, axis=1, keepdims=True) + epsilon)
    inverse_ref[...] = jnp.broadcast_to(inverse, (pixels, 128))
    normed_ref[...] = hsum * inverse
    lifted = normed_ref[...] * gain_ref[...].reshape(1, channels)
    act_ref[...] = (lifted * jax.nn.sigmoid(lifted)).astype(BF16)
    abuf[me] = act_ref[...].T
    acts = Gather(abuf, a_send, a_recv)
    acts.cross()
    acts.start(0)
    own = act_ref[...]
    sums = [dot(own, kernel_ref[3 + d]) for d in range(3)]
    acts.start(1)
    part = channels // 2
    half = pl.ds(pl.multiple_of(core * part, part), part)

    def shift_one(chunk):
        plain = abuf[chunk]
        values = plain.astype(F32)
        here = pl.ds(pl.multiple_of((chunk + 1) * pixels, pixels), pixels)
        shifted[0:channels, here] = moved(values, -1, 1).astype(BF16)
        shifted[channels : 2 * channels, here] = plain
        shifted[2 * channels : 3 * channels, here] = moved(values, 1, 1).astype(BF16)

    def shift_plane(order):
        base = acts.planes[order] * 4

        def step(i, carry):
            shift_one(base + i)
            return carry

        lax.fori_loop(0, 4, step, 0)

    def half_copy(row):
        return pltpu.make_async_remote_copy(
            src_ref=acc_ref.at[pl.ds(3 * row, 3), half],
            dst_ref=acc_ref.at[pl.ds(3 * row, 3), half],
            send_sem=half_send.at[row],
            recv_sem=half_recv.at[row],
            device_id={"tile": acts.sibling},
            device_id_type=MESH,
        )

    def multiply(order, row):
        base, count = acts.planes[order] * 4, 4
        right = gbuf[pl.ds(base, count)].reshape(count * pixels, channels)
        start = pl.multiple_of((base + row) * pixels, pixels)
        for d in range(3):
            rows = pl.ds(pl.multiple_of(d * channels + core * part, part), part)
            piece = dot(shifted[rows, pl.ds(start, count * pixels)], right)
            if order == 0:
                acc_ref[3 * row + d, half, :] = piece
            else:
                acc_ref[3 * row + d, half, :] = acc_ref[3 * row + d, half, :] + piece
        if order == 2:
            half_copy(row).start()

    def multiply_column(row):
        first = acts.planes[3] * 4 + 2 * acts.x
        right = gbuf[pl.ds(first, 2)].reshape(2 * pixels, channels)
        start = pl.multiple_of((first + row) * pixels, pixels)
        for d in range(3):
            left = shifted[d * channels : (d + 1) * channels, pl.ds(start, 2 * pixels)]
            acc_ref[3 * row + d] = acc_ref[3 * row + d] + dot(left, right)

    acts.relay(("X00", "Z10", "X01", "Z11"), ("X00", "Z10", "Z20", "X01", "Z11", "Z21"))
    acts.take(0)
    acts.take_cross()
    above = abuf[jnp.where(me > 0, me - 1, ZERO)].T
    below = abuf[jnp.where(me < 15, me + 1, ZERO)].T
    sums = [
        sums[d] + dot(above, kernel_ref[d]) + dot(below, kernel_ref[6 + d]) for d in range(3)
    ]
    predicted = sums[1] + moved(sums[0], -1, 0) + moved(sums[2], 1, 0)
    grad = (
        wide(pixel_weight)
        * (predicted - clean_ref[...].astype(F32) + noise_ref[...].astype(F32))
    ).astype(BF16)
    gbuf[me] = grad
    grads = Gather(gbuf, g_send, g_recv, False)
    grads.cross()
    grads.start(0)
    grads.start(1)
    own = gbuf[me]
    sums = [dot_back(own, kernel_ref[3 + d]) for d in range(3)]
    acts.relay(("Z20", "X10"), ("Z30", "X10", "X20"))
    acts.relay(("Z21", "X11"), ("Z31", "X11", "X21"))
    shift_plane(0)
    grads.relay(("X00", "Z10", "X01", "Z11"), ("X00", "Z10", "Z20", "X01", "Z11", "Z21"))
    grads.take(0)
    grads.take_cross()
    above = gbuf[jnp.where(me > 0, me - 1, ZERO)]
    below = gbuf[jnp.where(me < 15, me + 1, ZERO)]
    sums = [
        sums[d] + dot_back(below, kernel_ref[d]) + dot_back(above, kernel_ref[6 + d])
        for d in range(3)
    ]
    flows = sums[1] + moved(sums[0], 1, 0) + moved(sums[2], -1, 0)
    acts.relay(("Z30", "X20", "Z31", "X21"), ())
    acts.take(1)
    shift_plane(1)

    gain = gain_ref[...].reshape(1, channels)
    normed = normed_ref[...]
    lifted = normed * gain
    logistic = jax.nn.sigmoid(lifted)
    grad_lift = flows * logistic * (1.0 + lifted * (1.0 - logistic))
    gain_part = jnp.sum(grad_lift * normed, axis=0, keepdims=True)
    grad_norm = grad_lift * gain
    grad_hsum = wide(inverse_ref[...]) * (
        grad_norm - normed * jnp.mean(grad_norm * normed, axis=1, keepdims=True)
    )
    scaled = (grad_hsum * wide(inv_cov[...])).astype(BF16)
    cotangent_wide = dot(chosen[...], scaled)
    cotangent = cotangent_wide.astype(BF16)
    grad_hidden = cotangent_wide
    small_rows = []
    for k in range(3):
        grad_hidden = grad_hidden + dot_back(
            along_face(cotangent_wide, -2 * (k - 1)).astype(BF16), w2_dense[k]
        )
        product = jnp.where(keep2, dot(hiddens[k].T, cotangent), 0.0)
        small_rows.append(sum(product[48 * g : 48 * (g + 1)] for g in range(8)))
    logistic = jax.nn.sigmoid(first_out[...])
    grad_first = grad_hidden * logistic * (1.0 + first_out[...] * (1.0 - logistic))
    grad_high = grad_first.astype(BF16)
    grad_low = (grad_first - grad_high.astype(F32)).astype(BF16)
    for k in range(3):
        turned = inputs[k].T
        product = jnp.where(keep1, dot(turned, grad_high) + dot(turned, grad_low), 0.0)
        small_rows.append(sum(product[16 * g : 16 * (g + 1)] for g in range(8)))
    small_rows.append(
        jnp.where(iota((16, channels), 0) == 0, jnp.broadcast_to(gain_part, (16, channels)), 0.0)
    )
    small_out[...] = jnp.concatenate(small_rows, axis=0).astype(BF16)
    def small_send(k):
        to = lax.rem(me + k, 16)
        rows = pl.ds(pl.multiple_of(jnp.minimum(to, 12) * 16, 16), 16)
        return to < 13, pltpu.make_async_remote_copy(
            src_ref=small_out.at[rows],
            dst_ref=small_in.at[me],
            send_sem=s_send.at[k - 1],
            recv_sem=s_recv.at[k - 1],
            device_id={"tile": to},
            device_id_type=MESH,
        )

    my_rows = pl.ds(pl.multiple_of(jnp.minimum(me, 12) * 16, 16), 16)

    def small_spread(k):
        return pltpu.make_async_remote_copy(
            src_ref=small_ref.at[my_rows],
            dst_ref=small_ref.at[my_rows],
            send_sem=t_send.at[k - 1],
            recv_sem=t_recv.at[k - 1],
            device_id={"tile": lax.rem(me + k, 16)},
            device_id_type=MESH,
        )

    for k in range(1, 16):
        valid, send = small_send(k)

        @pl.when(valid)
        def _():
            send.start()

    grads.relay(("Z20", "X10"), ("Z30", "X10", "X20"))
    acts.relay(("X30", "X31"))
    acts.take(2)
    shift_plane(2)
    grads.relay(("Z21", "X11"), ("Z31", "X11", "X21"))
    multiply(0, 0)
    multiply(0, 1)
    acts.take(3)
    grads.relay(("Z30", "X20"), ())
    multiply(0, 2)
    shift_plane(3)
    grads.relay(("Z31", "X21"), ())
    grads.take(1)
    multiply(1, 0)

    multiply(1, 1)
    multiply(1, 2)
    grads.take(2)
    @pl.when(me < 13)
    def _():
        for k in range(1, 16):
            small_send(k)[1].wait_recv()
        small_in[me] = small_out[my_rows, :]
        added = small_in[0].astype(F32)
        for k in range(1, 16):
            added = added + small_in[k].astype(F32)
        small_ref[my_rows, :] = added.astype(BF16)
        for k in range(1, 16):
            small_spread(k).start()

    grads.relay(("X30",))
    multiply(2, 0)
    multiply(2, 1)
    multiply(2, 2)
    grads.take(3, (0,))
    half_copy(0).wait()
    multiply_column(0)
    half_copy(1).wait()
    multiply_column(1)
    grads.relay(("X31",))
    half_copy(2).wait()
    multiply_column(2)
    for k in range(1, 16):

        @pl.when(lax.rem(me + 16 - k, 16) < 13)
        def _():
            small_spread(k).wait_recv()

    grads.take(3, (1,))

    @pl.when(me < 13)
    def _():
        for k in range(1, 16):
            small_spread(k).wait_send()

    for k in range(1, 16):
        valid, send = small_send(k)

        @pl.when(valid)
        def _():
            send.wait_send()

    acts.drain()
    grads.drain()


def step_call(
    time_index, owner, slot, count, faces, mask, gain, first_w, second_w, clean, noise, kernel
):
    pixels, channels = clean.shape
    dma = pltpu.SemaphoreType.DMA
    whole = pl.BlockSpec(memory_space=VM)
    staged = (owner, slot, count, faces, mask, gain, first_w, second_w, clean, noise, kernel)
    staged = tuple(pltpu.with_memory_space_constraint(array, pltpu.HBM) for array in staged)
    return pl.pallas_call(
        step_kernel,
        out_shape=(
            jax.ShapeDtypeStruct((9, channels, channels), F32),
            jax.ShapeDtypeStruct((3 * channels, 18 * pixels), BF16),
            jax.ShapeDtypeStruct((17, pixels, channels), BF16),
            jax.ShapeDtypeStruct((208, channels), BF16),
        ),
        in_specs=[pl.BlockSpec(memory_space=pltpu.SMEM)]
        + [pl.BlockSpec(memory_space=ANY)] * len(staged),
        out_specs=(whole,) * 4,
        scratch_shapes=[VM(array.shape, array.dtype) for array in staged]
        + [
            dma((len(staged),)),
            VM((16, 32, 128), BF16),
            VM((16, 32, 128), BF16),
            dma((15,)),
            dma((15,)),
            VM((3, 128, channels), BF16),
            VM((3, channels, channels), BF16),
            VM((pixels, channels), F32),
            VM((256, channels), F32),
            VM((3, 256, 128), BF16),
            VM((3, 256, channels), BF16),
            VM((256, pixels), BF16),
            VM((pixels, 128), F32),
            VM((pixels, 128), F32),
            VM((pixels, channels), F32),
            VM((pixels, channels), BF16),
            VM((17, channels, pixels), BF16),
            dma((19 * PARTS,)),
            dma((16, PARTS)),
            dma((19 * PARTS,)),
            dma((16, PARTS)),
            VM((208, channels), BF16),
            VM((16, 16, channels), BF16),
            dma((15,)),
            dma((15,)),
            dma((15,)),
            dma((15,)),
            dma((3,)),
            dma((3,)),
        ],
        compiler_params=pltpu.CompilerParams(
            collective_id=0, has_side_effects=True, vmem_limit_bytes=28 * 2**20
        ),
        name="step",
    )(time_index, *staged)


def finish_kernel(
    acc_ref, shifted, gbuf, small_ref, kernel_out, gain_out, first_out, second_out, held, sems
):
    me = lax.axis_index("tile")
    channels = acc_ref.shape[1]
    pixels = gbuf.shape[1]
    z = me // 4
    base = 4 * jnp.where(z < 2, 3, 0) + 2 * (1 - lax.rem(me // 2, 2))
    right = gbuf[pl.ds(base, 2)].reshape(2 * pixels, channels)

    def step(row, carry):
        start = pl.multiple_of((base + row) * pixels, pixels)
        for d in range(3):
            tap = 3 * row + d
            left = shifted[d * channels : (d + 1) * channels, pl.ds(start, 2 * pixels)]
            held[tap] = acc_ref[tap] + dot(left, right)
            pltpu.make_async_copy(held.at[tap], kernel_out.at[tap], sems.at[tap]).start()
        return carry

    lax.fori_loop(0, 3, step, 0)
    summed = small_ref[...].astype(F32)
    for k in range(3):
        second = summed[48 * k : 48 * (k + 1)]
        first = summed[144 + 16 * k : 144 + 16 * (k + 1)]
        for g in range(8):
            turn = (channels - 48 * g) % channels
            turned = pltpu.roll(second, turn, 1)[:, :48] if turn else second[:, :48]
            second_out[(8 * k + g) * 48 : (8 * k + g + 1) * 48, :] = turned
            turned = pltpu.roll(first, turn, 1)[:, :48] if turn else first[:, :48]
            first_out[(8 * k + g) * 16 : (8 * k + g + 1) * 16, :] = turned
    gain_out[...] = summed[192]
    for tap in range(9):
        pltpu.make_async_copy(held.at[tap], kernel_out.at[tap], sems.at[tap]).wait()


def finish_call(acc, shifted, grads, small):
    channels = acc.shape[1]
    whole = pl.BlockSpec(memory_space=VM)
    return pl.pallas_call(
        finish_kernel,
        out_shape=(
            jax.ShapeDtypeStruct(acc.shape, F32),
            jax.ShapeDtypeStruct((channels,), F32),
            jax.ShapeDtypeStruct((384, 48), F32),
            jax.ShapeDtypeStruct((1152, 48), F32),
        ),
        in_specs=[whole] * 4,
        out_specs=(pl.BlockSpec(memory_space=ANY), whole, whole, whole),
        scratch_shapes=[VM(acc.shape, F32), pltpu.SemaphoreType.DMA((9,))],
        compiler_params=pltpu.CompilerParams(vmem_limit_bytes=12 * 2**20),
        name="finish",
    )(acc, shifted, grads, small)


def body16(
    sar_faces,
    dest_owner,
    face_slot,
    valid_pixels,
    cloud_mask,
    time_index,
    clean_latent,
    noise_latent,
    encoder_first,
    encoder_second,
    conv_kernel,
    norm_gain,
):
    channels_in = sar_faces.shape[-1]
    channels = clean_latent.shape[-1]
    acc, shifted, grads, small = step_call(
        time_index,
        dest_owner.reshape(1, -1),
        face_slot.reshape(1, -1),
        valid_pixels.reshape(1, -1),
        sar_faces.reshape(-1, channels_in),
        cloud_mask,
        norm_gain,
        encoder_first.reshape(-1, encoder_first.shape[-1]),
        encoder_second.reshape(-1, encoder_second.shape[-1]),
        clean_latent.reshape(-1, channels),
        noise_latent.reshape(-1, channels),
        conv_kernel,
    )
    grad_kernel, grad_gain, grad_first, grad_second = finish_call(acc, shifted, grads, small)
    return (
        grad_kernel,
        grad_gain,
        grad_first.reshape(encoder_first.shape),
        grad_second.reshape(encoder_second.shape),
    )


def body(
    sar_faces,
    dest_owner,
    face_slot,
    valid_pixels,
    cloud_mask,
    time_index,
    clean_latent,
    noise_latent,
    encoder_first,
    encoder_second,
    conv_kernel,
    norm_gain,
):
    owners = lax.axis_size("tile")
    slot_total = owners * MOST
    face_count, length, channels_in = sar_faces.shape
    rows, columns, channels = clean_latent.shape
    tile_faces = rows * columns // length
    owner_list = dest_owner[:, 0]
    order = jnp.arange(face_count, dtype=jnp.int32)
    within = jnp.sum(
        (
            (owner_list[:, None] == owner_list[None, :]) & (order[None, :] < order[:, None])
        ).astype(jnp.int32),
        axis=1,
    )
    buffer_at = owner_list * MOST + within
    placed = (jnp.arange(slot_total, dtype=jnp.int32)[:, None] == buffer_at[None, :]).astype(
        jnp.int32
    )
    placer = placed.astype(jnp.bfloat16)
    labels = jnp.stack(
        [
            jnp.sum(placed * face_slot[None, :], axis=1),
            jnp.sum(placed * valid_pixels[None, :], axis=1),
        ],
        axis=-1,
    )
    labels = labels.reshape(owners, MOST, 2)
    packed = jnp.einsum(
        "sf,fjc->sjc", placer, sar_faces, preferred_element_type=jnp.float32
    ).astype(jnp.bfloat16)
    arrived, recv_labels = (
        lax.all_to_all(
            packed.reshape(owners, MOST, length, channels_in),
            "tile",
            split_axis=0,
            concat_axis=0,
            tiled=True,
        ),
        lax.all_to_all(labels, "tile", split_axis=0, concat_axis=0, tiled=True),
    )
    raw_slots = arrived.reshape(slot_total, length, channels_in)
    received, saved = encoder_forward(raw_slots, encoder_first, encoder_second)
    recv_labels = recv_labels.reshape(slot_total, 2)
    recv_slot = recv_labels[:, 0]
    recv_count = recv_labels[:, 1]
    validity = (jnp.arange(length, dtype=jnp.int32)[None, :] < recv_count[:, None]).astype(
        jnp.float32
    )
    selector = recv_slot[:, None] == jnp.arange(tile_faces, dtype=jnp.int32)[None, :]
    masked = received * validity[..., None].astype(jnp.bfloat16)
    summed = jnp.einsum(
        "sp,sjc->pjc", selector.astype(jnp.bfloat16), masked, preferred_element_type=jnp.float32
    )
    covered = jnp.einsum(
        "sp,sj->pj", selector.astype(jnp.float32), validity, precision=highest
    ).reshape(-1, 1)
    condition = summed.reshape(-1, channels) / (1.0 + covered)
    time_value = (time_index[0].astype(jnp.float32) + 0.5) / NSTEPS
    noise_flat = noise_latent.astype(jnp.float32).reshape(-1, channels)
    clean_flat = clean_latent.astype(jnp.float32).reshape(-1, channels)
    hsum = (1.0 - time_value) * noise_flat + time_value * clean_flat + condition
    inverse = lax.rsqrt(jnp.mean(hsum * hsum, axis=-1, keepdims=True) + epsilon)
    normed = hsum * inverse
    lifted = normed * norm_gain
    activated = jax.nn.silu(lifted).astype(jnp.bfloat16).reshape(rows, columns, channels)
    extended = with_halo(activated, (("tile", 0),), 1)
    padded = jnp.pad(extended, ((0, 0), (1, 1), (0, 0)))
    predicted = convolve_forward(padded, conv_kernel, rows, columns)
    pixel_weight = (1 + cloud_mask).astype(jnp.float32).reshape(-1, 1)
    grad_pred = (pixel_weight * (predicted - clean_flat + noise_flat) / (rows * columns)).astype(
        jnp.bfloat16
    )
    grad_rows = with_halo(grad_pred.reshape(rows, columns, channels), (("tile", 0),), 1)
    padded_grad = jnp.pad(grad_rows, ((0, 0), (1, 1), (0, 0)))
    flows, kernel_part = convolve_backward(padded, padded_grad, conv_kernel, rows, columns)
    gain_part, grad_hsum = norm_backward(flows, lifted, normed, inverse, norm_gain)
    scaled = (grad_hsum / (1.0 + covered)).astype(jnp.bfloat16)
    target = recv_slot[:, None] * length + jnp.arange(length, dtype=jnp.int32)[None, :]
    target = jnp.where(validity > 0, target, -1).reshape(-1)
    picker = target[:, None] == jnp.arange(rows * columns, dtype=jnp.int32)[None, :]
    slot_grads = jnp.dot(
        picker.astype(jnp.bfloat16), scaled, preferred_element_type=jnp.float32
    ).astype(jnp.bfloat16)
    slot_grads = slot_grads.reshape(slot_total, length, channels)
    first_part, second_part = encoder_backward(saved, slot_grads, encoder_first, encoder_second)
    reduced = lax.psum((kernel_part, gain_part, first_part, second_part), "tile")
    return (reduced[0], reduced[1], reduced[2], reduced[3])


def solution(mesh):
    placed = (
        P(("groups", "tile"), None, None),
        P(("groups", "tile"), None),
        P(("groups", "tile")),
        P(("groups", "tile")),
        P(("groups", "tile"), None),
        P(("groups", "tile")),
        P(("groups", "tile"), None, None),
        P(("groups", "tile"), None, None),
        P(),
        P(),
        P(),
        P(),
    )
    return jax.shard_map(
        body16 if mesh.shape["tile"] == 16 else body,
        mesh=mesh,
        in_specs=placed,
        out_specs=(
            P("groups", None, None),
            P("groups"),
            P("groups", None, None, None),
            P("groups", None, None, None),
        ),
        check_vma=False,
    )
```
